128 devices in a mesh: tgt: 8 (over y_hi, z), ptr: 16 (over x, y_lo, core).
Axes of the slice: x: 4, y: 4 (y_hi: 2, y_lo: 2; y = y_hi * 2 + y_lo), z: 4, core: 2. Of those that a mesh axis runs over, the one named last changes fastest.
Arguments:
- targets: float32 [64, 32, 1024], P('tgt'), may hold values from -12 to 12
- partners: float32 [32, 32, 2048], P(None, None, 'ptr'), may hold values from -6 to 6
- occupied: int32 [16], P('ptr'), may hold values 0 or 1
- retained: int32 [1], replicated, may hold values from 32 to 64
Outputs:
- compressed: float32 [64, 32, 1024], P('tgt', 'ptr')
The draws below stay inside these ranges and needn't reach their ends.
All inputs are finite; a program needn't handle non-finite values. No bound on the sum of `occupied` on one device may be relied on, other than what follows from the above.
Results may differ from the reference program's by a relative error of at most 0.00008.
Values sent between devices are 32-bit elements; how exact they have to be, the bound alone decides.
No kernel may reach another device: no remote copies, remote signals or barrier semaphores. Data moves between devices by JAX's collectives and lax.ppermute only.
A program may use at most 64 MiB of HBM per device.

```python
import math
import jax
import jax.numpy as jnp
from jax import lax

NG = 32
NT = 64
NP = 64
NBLK = 16


def draw_targets(key, part):
    key_base = jax.random.fold_in(key, 11)
    key_mixing = jax.random.fold_in(key, 12)
    key_planes = jax.random.fold_in(key, 13)
    fields = jax.random.normal(key_base, (NT, NG, NG * NG), jnp.float32)
    mixing = 0.09 * jax.random.normal(key_mixing, (NT, NT), jnp.float32)
    mixing = mixing + jnp.eye(NT, dtype=jnp.float32)
    rising = jnp.arange(NG).astype(jnp.float32) / (NG - 1)
    envelope = jnp.exp(rising * 1.0986123) * jax.random.uniform(key_planes, (NG,), jnp.float32, 0.7, 1.4)
    mixed = jnp.einsum('ab,bxm->axm', mixing, fields, precision=jax.lax.Precision.HIGHEST)
    return jnp.clip(mixed * envelope[None, :, None], -12.0, 12.0)


def place_ends(array, stream_key, low, top_value):
    longest = array.shape.index(max(array.shape))
    spots = []
    for shift in (0, 1):
        where = [jax.random.randint(jax.random.fold_in(stream_key, axis), (), 0, length) for axis, length in enumerate(array.shape)]
        where[longest] = (where[longest] + shift) % array.shape[longest]
        spots.append(tuple(where))
    return array.at[spots[0]].set(low).at[spots[1]].set(top_value)


def shard_levels(own_key, extent, split, low, largest):
    loudness = 1.0
    for position, shards_of in split:
        draws = jax.random.uniform(jax.random.fold_in(jax.random.fold_in(own_key, 6), position), (shards_of,), jnp.float32, low / len(split), largest / len(split))
        loudness = loudness * jnp.repeat(jnp.exp(draws), extent[position] // shards_of).reshape((-1,) + (1,) * (len(extent) - 1 - position))
    return loudness


def scatter_about(stream_key, extent, width, reach, cuts=(), held_as=jnp.bfloat16):
    factor_of = shard_levels(stream_key, extent, cuts, -0.22, 0.18) if cuts else 1.0
    drawn = jax.random.normal(stream_key, extent, jnp.float32) * width * factor_of
    return jnp.minimum(jnp.maximum(drawn, -reach), reach).astype(held_as)


def setup_inputs(seed: int = 0) -> dict:
    seeds = jax.random.split(jax.random.key(seed), 5)
    return {
        "targets": draw_targets(jax.random.fold_in(seeds[4], 71), 0),
        "partners": scatter_about(seeds[1], (NG, NG, NP * NG), 1.0, 6.0, ((2, 16),), jnp.float32),
        "occupied": place_ends((jax.random.randint(seeds[2], (NBLK,), 0, 4) < 3).astype(jnp.int32), jax.random.fold_in(seeds[2], 1), 0, 1),
        "retained": jax.random.randint(seeds[3], (1,), NT // 2, NT + 1).astype(jnp.int32),
    }


def coulomb_table(length):
    indices = jnp.arange(length, dtype=jnp.int32)
    signed = jnp.where(indices < length // 2, indices, indices - length).astype(jnp.float32)
    wave = signed * (2.0 * math.pi / length)
    wave = wave * wave
    total = wave[:, None, None] + wave[None, :, None] + wave[None, None, :]
    safe = jnp.where(total > 0.0, total, jnp.float32(1.0))
    return jnp.where(total > 0.0, 4.0 * math.pi / safe, jnp.float32(0.0))

def reference(targets, partners, occupied, retained):
    ncells = NG * NG * NG
    coulomb = coulomb_table(NG)
    orbitals = jnp.transpose(partners.reshape(NG, NG, NP, NG), (2, 0, 1, 3))
    occupancy = 0.25 + 0.75 * jnp.repeat(occupied.astype(jnp.float32), 4)
    weighted = orbitals * occupancy[:, None, None, None]

    def action(target_one):
        density = target_one.reshape(NG, NG, NG)[None] * orbitals
        spectrum = jnp.fft.fftn(density, axes=(1, 2, 3))
        potential = jnp.real(jnp.fft.ifftn(spectrum * coulomb[None], axes=(1, 2, 3)))
        return jnp.sum(weighted * potential, axis=0).reshape(NG, NG * NG)
    actions = lax.map(action, targets)
    intersection = jnp.einsum('axm,bxm->ab', targets, actions, precision=lax.Precision.HIGHEST) / ncells
    lower = jnp.linalg.cholesky(intersection)
    inverse = jax.scipy.linalg.solve_triangular(lower, jnp.eye(NT, dtype=jnp.float32), lower=True)
    result = jnp.einsum('bc,cxm->bxm', inverse, actions, precision=lax.Precision.HIGHEST)
    keeping = (jnp.arange(NT, dtype=jnp.int32) < retained[0]).astype(jnp.float32)
    return result * keeping[:, None, None]
```

```python
import functools

import jax
import jax.numpy as jnp
import ml_dtypes
import numpy as np
from jax import lax
from jax.experimental import pallas as pl
from jax.experimental.pallas import tpu as pltpu
from jax.sharding import Mesh
from jax.sharding import PartitionSpec as P

TGT = ("tgt_0", "tgt_1")


HIGHEST_PRECISION = lax.Precision.HIGHEST


def cut_along(shard, dim, peers):
    before, after = (shard.shape[:dim], shard.shape[dim + 1 :])
    return jnp.moveaxis(shard.reshape(*before, peers, -1, *after), dim, 0)


def sent_and_summed(shard, axis, dim):
    peers = lax.axis_size(axis)
    blocks = lax.all_to_all(cut_along(shard, dim, peers), axis, 0, 0, tiled=True)
    return jnp.sum(blocks, axis=0)


def laid_out(blocks, dim):
    blocks = jnp.moveaxis(blocks, 0, dim)
    shape = blocks.shape
    return blocks.reshape(*shape[:dim], shape[dim] * shape[dim + 1], *shape[dim + 2 :])


def gather_in_order(shard, axes, sequence):
    blocks = shard[None]
    for k in sequence:
        blocks = lax.all_gather(blocks, axes[k], axis=0, tiled=True)
    carried = [lax.axis_size(axes[k]) for k in reversed(sequence)]
    blocks = blocks.reshape(*carried, *shard.shape)
    turned = sorted(range(len(sequence)), key=lambda place: sequence[len(sequence) - 1 - place])
    return blocks.transpose(*turned, *range(len(sequence), blocks.ndim)).reshape(-1, *shard.shape)


def whole_of(shard, axes, sequence, dim):
    return laid_out(gather_in_order(shard, axes, sequence), dim)


def copy_for_each(shard, axis):
    copies = jnp.broadcast_to(shard, (lax.axis_size(axis), *shard.shape))
    return lax.all_to_all(copies, axis, split_axis=0, concat_axis=0, tiled=True)


def of_everyone(shard, axis):
    return copy_for_each(shard, axis).sum(axis=0)


def gather_directly(shard, axis, dim):
    return laid_out(copy_for_each(shard, axis), dim)


def split_np(a):
    a = a.astype(np.float64)
    hi = a.astype(np.float32).astype(ml_dtypes.bfloat16)
    lo = (a - hi.astype(np.float64)).astype(np.float32).astype(ml_dtypes.bfloat16)
    return hi, lo

def half_bases(n):
    h = n // 2
    y = np.arange(h) + 0.5
    k = np.arange(h)
    even = np.cos(2 * np.pi * k[:, None] * y[None] / n) * np.sqrt(2.0 / h)
    even[0] *= np.sqrt(0.5)
    k = np.arange(1, h + 1)
    odd = np.sin(2 * np.pi * k[:, None] * y[None] / n) * np.sqrt(2.0 / h)
    odd[-1] *= np.sqrt(0.5)
    return (even, odd), (np.arange(h), np.arange(1, h + 1))

def tables(n, reps):
    bases, freqs = half_bases(n)
    lanes = []
    kern = []
    ix = np.arange(n)
    wx = np.where(ix < n // 2, ix, ix - n) * (2 * np.pi / n)
    for sy in (0, 1):
        for sz in (0, 1):
            m = np.einsum("ky,lz->yzkl", bases[sy], bases[sz]).reshape((n // 2) ** 2, (n // 2) ** 2)
            lanes.append(m)
            tot = (wx**2)[:, None, None] + ((freqs[sy] * 2 * np.pi / n) ** 2)[None, :, None] + ((freqs[sz] * 2 * np.pi / n) ** 2)[None, None, :]
            g = np.where(tot > 0, 4 * np.pi / np.where(tot > 0, tot, 1.0), 0.0) / 4
            kern.append(g.reshape(n, -1))
    lanes = np.stack(lanes)
    mh, ml = split_np(lanes)
    nh, nl = split_np(np.swapaxes(lanes, 1, 2))
    ph = 2 * np.pi * (ix[:, None] * ix[None] % n) / n
    cas = (np.cos(ph) + np.sin(ph)) / np.sqrt(n)
    w = np.kron(np.eye(reps), cas)
    wh, wl = split_np(w)
    lw = np.block([[wh, wh], [wl, np.zeros_like(wl)]])
    return (np.stack([mh, ml]), np.stack([nh, nl]), lw.astype(ml_dtypes.bfloat16), np.stack(kern).astype(np.float32))

def split(v):
    hi = v.astype(jnp.bfloat16)
    lo = (v - hi.astype(jnp.float32)).astype(jnp.bfloat16)
    return hi, lo

def dot(a, b):
    return jnp.dot(a, b, preferred_element_type=jnp.float32)

def lane_iota(rows):
    return lax.broadcasted_iota(jnp.int32, (rows, 128), 1)

def take(v, idx):
    return jnp.take_along_axis(v, idx, axis=1)

def fold_index(lane, sy, sz):
    yy = (lane // 16) % 4
    z = lane % 16
    return (3 - yy if sy else yy) * 32 + (31 - z if sz else z)

def unfold_index(lane, odd_tile, sy):
    yy = lane // 32
    z = lane % 32
    z = jnp.where(z >= 16, 31 - z, z)
    y8 = (4 if odd_tile else 0) + yy
    if sy:
        y8 = 7 - y8
    return y8 * 16 + z

def fold(tiles, rows):
    lane = lane_iota(rows)
    low = lane < 64
    out = {}
    for sy in (0, 1):
        for sz in (0, 1):
            idx = fold_index(lane, sy, sz)
            for h in (0, 1):
                a, b = (2 * h, 2 * h + 1) if sy == 0 else (7 - 2 * h, 6 - 2 * h)
                out[sy, sz, h] = jnp.where(low, take(tiles[a], idx), take(tiles[b], idx))
    return out

def unfold(folded, rows):
    lane = lane_iota(rows)
    low = lane % 32 < 16
    out = []
    for t in range(8):
        sy = t // 4
        h = t // 2 if sy == 0 else (7 - t) // 2
        odd = t % 2
        if sy == 0:
            idx = unfold_index(lane, odd, 0)
        else:
            yy = lane // 32
            z = lane % 32
            z = jnp.where(z >= 16, 31 - z, z)
            idx = ((7 if t % 2 == 0 else 3) - yy) * 16 + z
        out.append(jnp.where(low, take(folded[sy, 0, h], idx), take(folded[sy, 1, h], idx)))
    return out


def body(nj, tb, t_ref, p_ref, occ_ref, m_ref, n_ref, w_ref, k_ref, o_ref, pf, pw, tf, gh, gl, ust, ps):
    n = 32
    rows = nj * n

    @pl.when(pl.program_id(0) == 0)
    def _():
        lane = lane_iota(n)
        for j in range(nj):
            tiles = []
            for t in range(8):
                acc = None
                for yy in range(4):
                    src = p_ref[pl.ds(4 * t + yy, n, stride=n), :]
                    if yy != j:
                        src = pltpu.roll(src, ((yy - j) % 4) * n, 1)
                    acc = src if acc is None else jnp.where(lane // n == yy, src, acc)
                tiles.append(acc)
            f = fold(tiles, n)
            for (sy, sz, h), v in f.items():
                c = (2 * sy + sz) * 256 + h * 128
                pf[j * n:(j + 1) * n, c:c + 128] = v
                pw[j * n:(j + 1) * n, c:c + 128] = v * occ_ref[0, 0]

    for i in range(tb):
        f = fold([t_ref[i, :, 128 * t:128 * t + 128] for t in range(8)], n)
        for (sy, sz, h), v in f.items():
            c = (2 * sy + sz) * 256 + h * 128
            tf[:, c:c + 128] = v
        for j in range(nj):
            r = slice(j * n, (j + 1) * n)
            q = slice(i * rows + j * n, i * rows + (j + 1) * n)
            d = [tf[:, 256 * s:256 * s + 256] * pf[r, 256 * s:256 * s + 256] for s in range(4)]
            a, b, c, e = d[0] + d[1], d[0] - d[1], d[2] + d[3], d[2] - d[3]
            for s, g in enumerate((a + c, b + e, a - c, b - e)):
                hi, lo = split(g)
                gh[s, q, :] = hi
                gl[s, q, :] = lo
    for s in range(4):
        u = dot(gh[s], m_ref[0, s]) + dot(gl[s], m_ref[0, s]) + dot(gh[s], m_ref[1, s])
        for i in range(tb):
            hi, lo = split(u[i * rows:(i + 1) * rows])
            ust[0:rows, :] = hi
            ust[rows:2 * rows, :] = lo
            v = dot(w_ref[...], ust[...])
            v = (v[:rows] + v[rows:]).reshape(nj, n, 256) * k_ref[s][None]
            hi, lo = split(v.reshape(rows, 256))
            ust[0:rows, :] = hi
            ust[rows:2 * rows, :] = lo
            v = dot(w_ref[...], ust[...])
            v = v[:rows] + v[rows:]
            hi, lo = split(v)
            gh[s, i * rows:(i + 1) * rows, :] = hi
            gl[s, i * rows:(i + 1) * rows, :] = lo
        ps[s] = dot(gh[s], n_ref[0, s]) + dot(gl[s], n_ref[0, s]) + dot(gh[s], n_ref[1, s])
    for i in range(tb):
        acc = [None] * 4
        for j in range(nj):
            r = slice(j * n, (j + 1) * n)
            q = slice(i * rows + j * n, i * rows + (j + 1) * n)
            g = [ps[s, q, :] for s in range(4)]
            a, b, c, e = g[0] + g[1], g[0] - g[1], g[2] + g[3], g[2] - g[3]
            for s, v in enumerate((a + c, b + e, a - c, b - e)):
                v = v * pw[r, 256 * s:256 * s + 256]
                acc[s] = v if acc[s] is None else acc[s] + v
        folded = {(s // 2, s % 2, h): acc[s][:, 128 * h:128 * h + 128] for s in range(4) for h in (0, 1)}
        for t, v in enumerate(unfold(folded, n)):
            o_ref[i, :, 128 * t:128 * t + 128] = v

def exchange(targets, partners, occupied, tb=8):
    na, n, plane = targets.shape
    nj = partners.shape[2] // n
    m, mt, lw, kt = tables(n, nj)
    occ = (0.25 + 0.75 * occupied.astype(jnp.float32)).reshape(1, 1)
    rows = nj * n
    full = lambda a: pl.BlockSpec(a.shape, lambda i: (0,) * a.ndim)
    p2 = partners.reshape(n * n, nj * n)
    return pl.pallas_call(
        functools.partial(body, nj, tb),
        out_shape=jax.ShapeDtypeStruct(targets.shape, jnp.float32),
        grid=(na // tb,),
        in_specs=[pl.BlockSpec((tb, n, plane), lambda i: (i, 0, 0)), full(p2), pl.BlockSpec(memory_space=pltpu.SMEM), full(m), full(mt), full(lw), full(kt)],
        out_specs=pl.BlockSpec((tb, n, plane), lambda i: (i, 0, 0)),
        scratch_shapes=[
            pltpu.VMEM((rows, plane), jnp.float32),
            pltpu.VMEM((rows, plane), jnp.float32),
            pltpu.VMEM((n, plane), jnp.float32),
            pltpu.VMEM((4, tb * rows, plane // 4), jnp.bfloat16),
            pltpu.VMEM((4, tb * rows, plane // 4), jnp.bfloat16),
            pltpu.VMEM((2 * rows, plane // 4), jnp.bfloat16),
            pltpu.VMEM((4, tb * rows, plane // 4), jnp.float32),
        ],
        compiler_params=pltpu.CompilerParams(vmem_limit_bytes=48 << 20),
    )(targets, p2, occ, jnp.asarray(m), jnp.asarray(mt), jnp.asarray(lw), jnp.asarray(kt))


def shards(targets, partners, occupied, retained):
    length = targets.shape[1]
    owned_count = targets.shape[0]
    all_cells = length**3

    slab_count = length // lax.axis_size("ptr")
    slab_start = lax.axis_index("ptr") * slab_count
    every_action = exchange(targets, partners, occupied)
    action_slab = sent_and_summed(every_action, "ptr", 1)
    own_slab = lax.dynamic_slice_in_dim(targets, slab_start, slab_count, 1)
    target_slab = whole_of(own_slab, TGT, (0, 1), 0)
    total_targets = target_slab.shape[0]
    columns = (
        jnp.einsum("asm,bsm->ab", target_slab, action_slab, precision=HIGHEST_PRECISION) / all_cells
    )
    first_owned = lax.axis_index(TGT) * owned_count
    summed_columns = of_everyone(columns, "ptr")
    intersection = gather_directly(summed_columns, TGT, 1)
    lower = jnp.linalg.cholesky(intersection)
    inverse = jax.scipy.linalg.solve_triangular(
        lower, jnp.eye(total_targets, dtype=jnp.float32), lower=True
    )
    all_actions = gather_directly(action_slab, TGT, 0)
    own_rows = lax.dynamic_slice_in_dim(inverse, first_owned, owned_count, 0)
    result = jnp.einsum("bc,csm->bsm", own_rows, all_actions, precision=HIGHEST_PRECISION)
    global_rows = first_owned + jnp.arange(owned_count, dtype=jnp.int32)
    keeping = (global_rows < retained[0]).astype(jnp.float32)
    return result * keeping[:, None, None]


def solution(mesh):
    finer = Mesh(mesh.devices.reshape(2, 4, mesh.shape["ptr"]), ("tgt_0", "tgt_1", "ptr"))
    in_specs = (P(TGT, None, None), P(None, None, "ptr"), P("ptr"), P())
    out_specs = P(TGT, "ptr", None)
    return jax.shard_map(
        shards, mesh=finer, in_specs=in_specs, out_specs=out_specs, check_vma=False
    )
```

```python
import functools

import jax
import jax.numpy as jnp
import ml_dtypes
import numpy as np
from jax import lax
from jax.experimental import pallas as pl
from jax.experimental.pallas import tpu as pltpu
from jax.sharding import Mesh
from jax.sharding import PartitionSpec as P

TGT = ("tgt_0", "tgt_1")
PTR = ("ptr_0", "ptr_1", "core")
SLABS = ("ptr_0", "ptr_1")
LANES = 128


def split_np(a):
    a = a.astype(np.float64)
    hi = a.astype(np.float32).astype(ml_dtypes.bfloat16)
    lo = (a - hi.astype(np.float64)).astype(np.float32).astype(ml_dtypes.bfloat16)
    return hi, lo


def half_bases(n):
    h = n // 2
    y = np.arange(h) + 0.5
    even_k, odd_k = np.arange(h), np.arange(1, h + 1)
    even = np.cos(2 * np.pi * even_k[:, None] * y[None] / n) * np.sqrt(2.0 / h)
    even[0] *= np.sqrt(0.5)
    odd = np.sin(2 * np.pi * odd_k[:, None] * y[None] / n) * np.sqrt(2.0 / h)
    odd[-1] *= np.sqrt(0.5)
    return (even, odd), (even_k, odd_k)


def tables(n, reps):
    bases, freqs = half_bases(n)
    planes, kernels = [], []
    ix = np.arange(n)
    wave = lambda k: (k * (2 * np.pi / n)) ** 2
    wx = wave(np.where(ix < n // 2, ix, ix - n))
    for sy in (0, 1):
        for sz in (0, 1):
            m = np.einsum("ky,lz->yzkl", bases[sy], bases[sz])
            planes.append(m.reshape(n * n // 4, n * n // 4))
            total = wx[:, None, None] + wave(freqs[sy])[:, None] + wave(freqs[sz])[None]
            g = np.where(total > 0, 4 * np.pi / np.where(total > 0, total, 1.0), 0.0)
            kernels.append(g.reshape(n, -1) / 4)
    planes = np.stack(planes)
    phase = 2 * np.pi * (ix[:, None] * ix[None] % n) / n
    wh, wl = split_np(np.kron(np.eye(reps), (np.cos(phase) + np.sin(phase)) / np.sqrt(n)))
    left = np.block([[wh, wh], [wl, np.zeros_like(wl)]]).astype(ml_dtypes.bfloat16)
    forward = np.stack(split_np(planes))
    back = np.stack(split_np(np.swapaxes(planes, 1, 2)))
    return forward, back, left, np.stack(kernels).astype(np.float32)


def split(v):
    hi = v.astype(jnp.bfloat16)
    return hi, (v - hi.astype(jnp.float32)).astype(jnp.bfloat16)


def dot(a, b):
    return jnp.dot(a, b, preferred_element_type=jnp.float32)


def take(v, idx):
    return jnp.take_along_axis(v, idx, axis=1)


def fold(tiles, rows):
    lane = lax.broadcasted_iota(jnp.int32, (rows, LANES), 1)
    y, z = (lane // 16) % 4, lane % 16
    out = {}
    for sy in (0, 1):
        for sz in (0, 1):
            idx = (3 - y if sy else y) * 32 + (31 - z if sz else z)
            for h in (0, 1):
                a, b = (7 - 2 * h, 6 - 2 * h) if sy else (2 * h, 2 * h + 1)
                out[2 * sy + sz, h] = jnp.where(lane < 64, take(tiles[a], idx), take(tiles[b], idx))
    return out


def unfold(folded, rows):
    lane = lax.broadcasted_iota(jnp.int32, (rows, LANES), 1)
    y, z = lane // 32, lane % 32
    low = z < 16
    z = jnp.where(low, z, 31 - z)
    out = []
    for t in range(8):
        sy = t // 4
        h = (7 - t) // 2 if sy else t // 2
        first = 7 - 4 * (t % 2) if sy else 4 * (t % 2)
        idx = (first - y if sy else first + y) * 16 + z
        out.append(jnp.where(low, take(folded[2 * sy, h], idx), take(folded[2 * sy + 1, h], idx)))
    return out


def butterfly(d):
    a, b, c, e = d[0] + d[1], d[0] - d[1], d[2] + d[3], d[2] - d[3]
    return a + c, b + e, a - c, b - e


def solve_body(last, tb, nj, n, *refs):
    if last:
        t_ref, prior, p_ref, occ_ref, m_hbm, b_hbm, w_hbm, k_hbm, o_ref = refs[:9]
    else:
        t_hbm, p_ref, occ_ref, m_hbm, b_hbm, w_hbm, k_hbm, o_ref, tf_out = refs[:9]
    pbuf, pf, pw, mw, bw, ww, kw, tbuf, gh, gl, ust, ps, sems = refs[9:]
    rows, quarter = nj * n, n * n // 4
    copies = [
        pltpu.make_async_copy(src, dst, sems.at[i])
        for i, (src, dst) in enumerate(
            ((p_ref, pbuf), (m_hbm, mw), (w_hbm, ww), (k_hbm, kw), (b_hbm, bw))
        )
    ]
    if last:
        copies.append(pltpu.make_async_copy(t_ref, tbuf, sems.at[5]))
    else:
        mine = pl.ds(lax.axis_index("core") * tb, tb)
        copies.append(pltpu.make_async_copy(t_hbm.at[mine], tbuf, sems.at[5]))
    for i in (0, 5, 1, 2, 3, 4):
        copies[i].start()
    copies[0].wait()
    lane = lax.broadcasted_iota(jnp.int32, (n, LANES), 1)
    for j in range(nj):
        tiles = []
        for t in range(8):
            acc = None
            for y in range(4):
                src = pbuf[pl.ds(4 * t + y, n, stride=n), :]
                if y != j:
                    src = pltpu.roll(src, ((y - j) % 4) * n, 1)
                acc = src if acc is None else jnp.where(lane // n == y, src, acc)
            tiles.append(acc)
        for (s, h), v in fold(tiles, n).items():
            at = slice(s * quarter + h * LANES, s * quarter + (h + 1) * LANES)
            pf[j * n : (j + 1) * n, at] = v
            pw[j * n : (j + 1) * n, at] = v * occ_ref[0, 0]
    copies[5].wait()
    for i in range(tb):
        if not last:
            tiles = [tbuf[i, :, LANES * t : LANES * (t + 1)] for t in range(8)]
            for (s, h), v in fold(tiles, n).items():
                tf_out[i, :, s * quarter + h * LANES : s * quarter + (h + 1) * LANES] = v
        tf = tbuf if last else tf_out
        for j in range(nj):
            r = slice(j * n, (j + 1) * n)
            q = slice(i * rows + j * n, i * rows + (j + 1) * n)
            d = [
                tf[i, :, quarter * s : quarter * (s + 1)] * pf[r, quarter * s : quarter * (s + 1)]
                for s in range(4)
            ]
            for s, g in enumerate(butterfly(d)):
                gh[s, q, :], gl[s, q, :] = split(g)
    for i in (1, 2, 3, 4):
        copies[i].wait()
    for s in range(4):
        u = dot(gh[s], mw[0, s]) + dot(gl[s], mw[0, s]) + dot(gh[s], mw[1, s])
        for i in range(tb):
            at = slice(i * rows, (i + 1) * rows)
            ust[i, :rows, :], ust[i, rows:, :] = split(u[at])
            v = dot(ww[...], ust[i])
            v = (v[:rows] + v[rows:]).reshape(nj, n, quarter) * kw[s][None]
            ust[i, :rows, :], ust[i, rows:, :] = split(v.reshape(rows, quarter))
            v = dot(ww[...], ust[i])
            gh[s, at, :], gl[s, at, :] = split(v[:rows] + v[rows:])
        ps[s] = dot(gh[s], bw[0, s]) + dot(gl[s], bw[0, s]) + dot(gh[s], bw[1, s])
    for i in range(tb):
        acc = [prior[i, :, quarter * s : quarter * (s + 1)] if last else None for s in range(4)]
        for j in range(nj):
            r = slice(j * n, (j + 1) * n)
            q = slice(i * rows + j * n, i * rows + (j + 1) * n)
            for s, v in enumerate(butterfly([ps[s, q, :] for s in range(4)])):
                v = v * pw[r, quarter * s : quarter * (s + 1)]
                acc[s] = v if acc[s] is None else acc[s] + v
        if last:
            folded = {(s, h): acc[s][:, LANES * h : LANES * (h + 1)] for s in range(4) for h in (0, 1)}
            peers = o_ref.shape[0]
            each = n // peers
            for t, v in enumerate(unfold(folded, n)):
                for d in range(peers):
                    o_ref[d, i * each : (i + 1) * each, LANES * t : LANES * (t + 1)] = v[
                        d * each : (d + 1) * each
                    ]
        else:
            for s in range(4):
                o_ref[i, :, quarter * s : quarter * (s + 1)] = acc[s]


def solve(targets, partners, occupied, consts, prior=None, peers=8):
    last = prior is not None
    n = 32
    nj = partners.shape[1] // n
    tb = prior.shape[0] if last else targets.shape[0] // 2
    rows, quarter = nj * n, n * n // 4
    forward, back, left, kernel = consts
    occ = (0.25 + 0.75 * occupied.astype(jnp.float32)).reshape(1, 1)
    hbm = pl.BlockSpec(memory_space=pl.ANY)
    vmem = pl.BlockSpec(memory_space=pltpu.VMEM)
    smem = pl.BlockSpec(memory_space=pltpu.SMEM)
    part = jax.ShapeDtypeStruct((tb, n, n * n), jnp.float32)
    if last:
        operands = (targets, prior)
        out_shape = jax.ShapeDtypeStruct((peers, tb * n // peers, n * n), jnp.float32)
        in_specs, out_specs = [hbm, vmem, hbm, smem, hbm, hbm, hbm, hbm], vmem
    else:
        operands = (targets,)
        out_shape = (part, part)
        in_specs, out_specs = [hbm, hbm, smem, hbm, hbm, hbm, hbm], (vmem, vmem)
    return pl.pallas_call(
        functools.partial(solve_body, last, tb, nj, n),
        out_shape=out_shape,
        in_specs=in_specs,
        out_specs=out_specs,
        scratch_shapes=[
            pltpu.VMEM(partners.shape, jnp.float32),
            pltpu.VMEM((rows, n * n), jnp.float32),
            pltpu.VMEM((rows, n * n), jnp.float32),
            pltpu.VMEM(forward.shape, jnp.bfloat16),
            pltpu.VMEM(back.shape, jnp.bfloat16),
            pltpu.VMEM(left.shape, jnp.bfloat16),
            pltpu.VMEM(kernel.shape, jnp.float32),
            pltpu.VMEM(part.shape, jnp.float32),
            pltpu.VMEM((4, tb * rows, quarter), jnp.bfloat16),
            pltpu.VMEM((4, tb * rows, quarter), jnp.bfloat16),
            pltpu.VMEM((tb, 2 * rows, quarter), jnp.bfloat16),
            pltpu.VMEM((4, tb * rows, quarter), jnp.float32),
            pltpu.SemaphoreType.DMA((6,)),
        ],
        compiler_params=pltpu.CompilerParams(vmem_limit_bytes=48 << 20),
        cost_estimate=pl.CostEstimate(
            flops=2 * 5 * tb * 4 * rows * quarter * quarter, bytes_accessed=8 << 20, transcendentals=0
        ),
    )(*operands, partners, occ, forward, back, left, kernel)


def spread_body(copies, in_ref, o_ref):
    peers, rows, _ = in_ref.shape
    total = in_ref[0]
    for k in range(1, peers):
        total = total + in_ref[k]
    each = 4
    for core in (0, 1):
        picked = jnp.concatenate(
            [
                total[i * each + 2 * core + q : i * each + 2 * core + q + 1]
                for q in (0, 1)
                for i in range(rows // each)
            ],
            axis=0,
        )
        for k in range(copies):
            o_ref[2 * k + core] = picked


def spread(received, copies):
    _, rows, plane = received.shape
    return pl.pallas_call(
        functools.partial(spread_body, copies),
        out_shape=jax.ShapeDtypeStruct((2 * copies, rows // 2, plane), jnp.float32),
        compiler_params=pltpu.CompilerParams(vmem_limit_bytes=16 << 20),
    )(received)


def plane_of(ref, q):
    return jnp.concatenate([ref[8 * g + 4 * q : 8 * g + 4 * q + 4, :] for g in range(ref.shape[0] // 8)], axis=0)


def overlap_body(scale, t_ref, a_ref, o_ref):
    half = t_ref.shape[0] // 2
    total = None
    for q in (0, 1):
        s = lax.dot_general(
            plane_of(t_ref, q),
            plane_of(a_ref, q),
            (((1,), (1,)), ((), ())),
            precision=lax.Precision.HIGHEST,
            preferred_element_type=jnp.float32,
        )
        total = s if total is None else total + s
    total = total * scale
    packed = jnp.concatenate([total[: half // 2], total[half // 2 :]], axis=1)
    for k in range(o_ref.shape[0]):
        o_ref[k] = packed


def overlap(target_slab, action_slab, copies, scale):
    half = target_slab.shape[0] // 2
    return pl.pallas_call(
        functools.partial(overlap_body, scale),
        out_shape=jax.ShapeDtypeStruct((copies, half // 2, 2 * half), jnp.float32),
        compiler_params=pltpu.CompilerParams(vmem_limit_bytes=16 << 20),
    )(target_slab, action_slab)


def compress_body(owned, s_ref, a_ref, keep_ref, o_ref, inv_ref):
    total = s_ref[0]
    for k in range(1, s_ref.shape[0]):
        total = total + s_ref[k]
    half = total.shape[0]
    count = 2 * half
    square = jnp.concatenate([total[:, :count], total[:, count:]], axis=0)
    square = 0.5 * (square + square.T)
    row = lax.broadcasted_iota(jnp.int32, (count, count), 0)
    col = lax.broadcasted_iota(jnp.int32, (count, count), 1)
    wide = jnp.concatenate([square, jnp.where(row == col, 1.0, 0.0)], axis=1)
    tiles = [wide[8 * t : 8 * t + 8] for t in range(count // 8)]
    sub = lax.broadcasted_iota(jnp.int32, (8, LANES), 0)
    down = lambda v, k: jnp.broadcast_to(v[k : k + 1], (8, LANES))
    for p in range(count // 8):
        later = range(p, count // 8)
        cols = {
            (t, k): jnp.broadcast_to(tiles[t][:, 8 * p + k : 8 * p + k + 1], (8, LANES))
            for t in later
            for k in range(8)
        }
        root = jnp.ones((8, LANES), jnp.float32)
        for k in range(8):
            pivot = down(cols[p, k], k)
            over = 1.0 / pivot
            root = jnp.where(sub == k, lax.rsqrt(pivot), root)
            line = down(tiles[p], k)
            cross = [down(cols[p, m], k) for m in range(k + 1, 8)]
            for t in later:
                f = cols[t, k] * over
                if t == p:
                    f = jnp.where(sub > k, f, 0.0)
                tiles[t] = tiles[t] - f * line
                for m in range(k + 1, 8):
                    cols[t, m] = cols[t, m] - f * cross[m - k - 1]
        inv_ref[8 * p : 8 * p + 8, :] = tiles[p] * root
    first = lax.axis_index(TGT) * owned
    mine = inv_ref[pl.ds(pl.multiple_of(first, 8), owned), :][:, count:]
    kept = first + lax.broadcasted_iota(jnp.int32, (owned, count), 0) < keep_ref[0]
    mine = jnp.where(kept, mine, 0.0)
    for q in (0, 1):
        o_ref[:, q, :] = jnp.dot(
            mine,
            plane_of(a_ref, q),
            precision=lax.Precision.HIGHEST,
            preferred_element_type=jnp.float32,
        )


def compress(summands, action_slab, retained, owned):
    count = action_slab.shape[0] // 2
    vmem = pl.BlockSpec(memory_space=pltpu.VMEM)
    return pl.pallas_call(
        functools.partial(compress_body, owned),
        out_shape=jax.ShapeDtypeStruct((owned, 2, action_slab.shape[1]), jnp.float32),
        in_specs=[vmem, vmem, pl.BlockSpec(memory_space=pltpu.SMEM)],
        out_specs=vmem,
        scratch_shapes=[pltpu.VMEM((count, LANES), jnp.float32)],
        compiler_params=pltpu.CompilerParams(vmem_limit_bytes=16 << 20),
    )(summands, action_slab, retained)


def gathered(shard, axes):
    for name in reversed(axes):
        shard = lax.all_gather(shard, name, axis=0, tiled=True)
    return shard


def shards(targets, partners, occupied, retained):
    owned, n, plane = targets.shape
    consts = [jnp.asarray(c) for c in tables(n, partners.shape[2] // n)]
    partners = partners.reshape(n * n, -1)
    swap = [(0, 1), (1, 0)]
    other_partners = lax.ppermute(partners, "core", swap)
    other_occupied = lax.ppermute(occupied.astype(jnp.float32), "core", swap)
    thick = n // lax.axis_size(PTR)
    first_plane = lax.axis_index(PTR) * thick
    own_slab = lax.dynamic_slice_in_dim(targets, first_plane, thick, 1)
    own_slab = own_slab.reshape(2, -1, thick, plane).transpose(0, 2, 1, 3).reshape(-1, plane)
    target_slab = gathered(own_slab, TGT)
    partial_actions, folded = solve(targets, partners, occupied, consts)
    cut = solve(folded, other_partners, other_occupied, consts, partial_actions, lax.axis_size(SLABS))
    received = lax.all_to_all(cut, SLABS, 0, 0, tiled=True)
    copies = spread(received, lax.axis_size(TGT))
    action_slab = lax.all_to_all(copies, TGT + ("core",), 0, 0, tiled=True).reshape(-1, plane)
    summands = overlap(target_slab, action_slab, lax.axis_size(PTR), 1.0 / n**3)
    summands = lax.all_to_all(summands, PTR, 0, 0, tiled=True)
    return compress(summands, action_slab, retained, owned)


def solution(mesh):
    names = TGT + PTR
    finer = Mesh(mesh.devices.reshape(2, 4, 4, 2, 2), names)
    in_specs = (P(TGT, None, None), P(None, None, PTR), P(PTR), P())
    out_specs = P(TGT, PTR, None)
    return jax.shard_map(
        shards, mesh=finer, in_specs=in_specs, out_specs=out_specs, check_vma=False
    )
```

```python
import functools

import jax
import jax.numpy as jnp
import ml_dtypes
import numpy as np
from jax import lax
from jax.experimental import pallas as pl
from jax.experimental.pallas import tpu as pltpu
from jax.sharding import Mesh
from jax.sharding import PartitionSpec as P

TGT = ("tgt_0", "tgt_1")
PTR = ("ptr_0", "ptr_1", "core")
SLABS = ("ptr_0", "ptr_1")
LANES = 128
SOLVE_PARAMS = pltpu.CompilerParams(vmem_limit_bytes=24 << 20)
SMALL_PARAMS = pltpu.CompilerParams(vmem_limit_bytes=16 << 20)


def split_np(a):
    a = a.astype(np.float64)
    hi = a.astype(np.float32).astype(ml_dtypes.bfloat16)
    lo = (a - hi.astype(np.float64)).astype(np.float32).astype(ml_dtypes.bfloat16)
    return hi, lo


def half_bases(n):
    h = n // 2
    y = np.arange(h) + 0.5
    even_k, odd_k = np.arange(h), np.arange(1, h + 1)
    even = np.cos(2 * np.pi * even_k[:, None] * y[None] / n) * np.sqrt(2.0 / h)
    even[0] *= np.sqrt(0.5)
    odd = np.sin(2 * np.pi * odd_k[:, None] * y[None] / n) * np.sqrt(2.0 / h)
    odd[-1] *= np.sqrt(0.5)
    return (even, odd), (even_k, odd_k)


def tables(n, reps):
    bases, freqs = half_bases(n)
    planes, kernels = [], []
    ix = np.arange(n)
    wave = lambda k: (k * (2 * np.pi / n)) ** 2
    wx = wave(np.where(ix < n // 2, ix, ix - n))
    for sy in (0, 1):
        for sz in (0, 1):
            m = np.einsum("ky,lz->yzkl", bases[sy], bases[sz])
            planes.append(m.reshape(n * n // 4, n * n // 4))
            total = wx[:, None, None] + wave(freqs[sy])[:, None] + wave(freqs[sz])[None]
            g = np.where(total > 0, 4 * np.pi / np.where(total > 0, total, 1.0), 0.0)
            kernels.append(g.reshape(n, -1) / 4)
    planes = np.stack(planes)
    phase = 2 * np.pi * (ix[:, None] * ix[None] % n) / n
    wh, wl = split_np(np.kron(np.eye(reps), (np.cos(phase) + np.sin(phase)) / np.sqrt(n)))
    left = np.block([[wh, wh], [wl, np.zeros_like(wl)]]).astype(ml_dtypes.bfloat16)
    matrices = [*split_np(planes), *split_np(np.swapaxes(planes, 1, 2)), left[None]]
    return np.concatenate(matrices), np.stack(kernels).astype(np.float32)


def split(v):
    hi = v.astype(jnp.bfloat16)
    return hi, (v - hi.astype(jnp.float32)).astype(jnp.bfloat16)


def dot(a, b):
    return jnp.dot(a, b, preferred_element_type=jnp.float32)


def take(v, idx):
    return jnp.take_along_axis(v, idx, axis=1)


def fold(tiles, rows):
    lane = lax.broadcasted_iota(jnp.int32, (rows, LANES), 1)
    y, z = (lane // 16) % 4, lane % 16
    out = {}
    for sy in (0, 1):
        for sz in (0, 1):
            idx = (3 - y if sy else y) * 32 + (31 - z if sz else z)
            for h in (0, 1):
                a, b = (7 - 2 * h, 6 - 2 * h) if sy else (2 * h, 2 * h + 1)
                out[2 * sy + sz, h] = jnp.where(lane < 64, take(tiles[a], idx), take(tiles[b], idx))
    return out


def unfold(folded, rows):
    lane = lax.broadcasted_iota(jnp.int32, (rows, LANES), 1)
    y, z = lane // 32, lane % 32
    low = z < 16
    z = jnp.where(low, z, 31 - z)
    out = []
    for t in range(8):
        sy = t // 4
        h = (7 - t) // 2 if sy else t // 2
        first = 7 - 4 * (t % 2) if sy else 4 * (t % 2)
        idx = (first - y if sy else first + y) * 16 + z
        out.append(jnp.where(low, take(folded[2 * sy, h], idx), take(folded[2 * sy + 1, h], idx)))
    return out


def butterfly(d):
    a, b, c, e = d[0] + d[1], d[0] - d[1], d[2] + d[3], d[2] - d[3]
    return a + c, b + e, a - c, b - e


def fold_body(nj, n, p_ref, occ_hbm, keep_hbm, o_ref, keep_ref, scalars, sems):
    copies = [
        pltpu.make_async_copy(src, scalars.at[i], sems.at[i]) for i, src in enumerate((occ_hbm, keep_hbm))
    ]
    for copy in copies:
        copy.start()
    for copy in copies:
        copy.wait()
    keep_ref[...] = jnp.full(keep_ref.shape, scalars[1, 0], jnp.int32)
    occ = jnp.full((n, LANES), scalars[0, 0], jnp.int32).astype(jnp.float32)
    root = jnp.sqrt(0.25 + 0.75 * occ)
    quarter = n * n // 4
    lane = lax.broadcasted_iota(jnp.int32, (n, LANES), 1)
    for j in range(nj):
        tiles = []
        for t in range(8):
            acc = None
            for y in range(4):
                src = p_ref[pl.ds(4 * t + y, n, stride=n), :]
                if y != j:
                    src = pltpu.roll(src, ((y - j) % 4) * n, 1)
                acc = src if acc is None else jnp.where(lane // n == y, src, acc)
            tiles.append(acc * root)
        for (s, h), v in fold(tiles, n).items():
            o_ref[j * n : (j + 1) * n, s * quarter + h * LANES : s * quarter + (h + 1) * LANES] = v


def folded_partners(partners, occupied, retained):
    n = partners.shape[0]
    nj = partners.shape[2] // n
    vmem = pl.BlockSpec(memory_space=pltpu.VMEM)
    hbm = pl.BlockSpec(memory_space=pltpu.HBM)
    return pl.pallas_call(
        functools.partial(fold_body, nj, n),
        out_shape=(
            jax.ShapeDtypeStruct((nj * n, n * n), jnp.float32),
            jax.ShapeDtypeStruct((8, LANES), jnp.int32),
        ),
        in_specs=[vmem, hbm, hbm],
        out_specs=(vmem, vmem),
        scratch_shapes=[pltpu.SMEM((2, 1), jnp.int32), pltpu.SemaphoreType.DMA((2,))],
        compiler_params=SMALL_PARAMS,
        cost_estimate=pl.CostEstimate(flops=2 << 30, bytes_accessed=8 << 20, transcendentals=0),
    )(partners.reshape(n * n, -1), occupied, retained)


def solve_body(last, tb, nj, n, *refs):
    if last:
        tf, prior, pf, w_ref, k_ref, o_ref = refs[:6]
    else:
        t_ref, pf, w_ref, k_ref, o_ref, tf = refs[:6]
    gh, gl, ust, ps = refs[6:]
    rows, quarter = nj * n, n * n // 4
    if not last:
        first = lax.axis_index("core") * tb
        for i in range(tb):
            tiles = [t_ref[first + i, :, LANES * t : LANES * (t + 1)] for t in range(8)]
            for (s, h), v in fold(tiles, n).items():
                tf[i, :, s * quarter + h * LANES : s * quarter + (h + 1) * LANES] = v
    for i in range(tb):
        for j in range(nj):
            r = slice(j * n, (j + 1) * n)
            q = slice(i * rows + j * n, i * rows + (j + 1) * n)
            d = [
                tf[i, :, quarter * s : quarter * (s + 1)] * pf[r, quarter * s : quarter * (s + 1)]
                for s in range(4)
            ]
            for s, g in enumerate(butterfly(d)):
                gh[s, q, :], gl[s, q, :] = split(g)
    left = w_ref[16]
    for s in range(4):
        mh, ml, bh, bl = (w_ref[4 * k + s] for k in range(4))
        u = dot(gh[s], mh) + dot(gl[s], mh) + dot(gh[s], ml)
        for i in range(tb):
            at = slice(i * rows, (i + 1) * rows)
            ust[i, :rows, :], ust[i, rows:, :] = split(u[at])
            v = dot(left, ust[i])
            v = (v[:rows] + v[rows:]).reshape(nj, n, quarter) * k_ref[s][None]
            ust[i, :rows, :], ust[i, rows:, :] = split(v.reshape(rows, quarter))
            v = dot(left, ust[i])
            gh[s, at, :], gl[s, at, :] = split(v[:rows] + v[rows:])
        ps[s] = dot(gh[s], bh) + dot(gl[s], bh) + dot(gh[s], bl)
    for i in range(tb):
        acc = [prior[i, :, quarter * s : quarter * (s + 1)] if last else None for s in range(4)]
        for j in range(nj):
            r = slice(j * n, (j + 1) * n)
            q = slice(i * rows + j * n, i * rows + (j + 1) * n)
            for s, v in enumerate(butterfly([ps[s, q, :] for s in range(4)])):
                v = v * pf[r, quarter * s : quarter * (s + 1)]
                acc[s] = v if acc[s] is None else acc[s] + v
        if last:
            folded = {(s, h): acc[s][:, LANES * h : LANES * (h + 1)] for s in range(4) for h in (0, 1)}
            peers = o_ref.shape[0]
            each = n // peers
            for t, v in enumerate(unfold(folded, n)):
                for d in range(peers):
                    o_ref[d, i * each : (i + 1) * each, LANES * t : LANES * (t + 1)] = v[
                        d * each : (d + 1) * each
                    ]
        else:
            for s in range(4):
                o_ref[i, :, quarter * s : quarter * (s + 1)] = acc[s]


def solve(targets, partners, consts, prior=None, peers=8):
    last = prior is not None
    n = targets.shape[1]
    nj = partners.shape[0] // n
    tb = prior.shape[0] if last else targets.shape[0] // 2
    rows, quarter = nj * n, n * n // 4
    vmem = pl.BlockSpec(memory_space=pltpu.VMEM)
    part = jax.ShapeDtypeStruct((tb, n, n * n), jnp.float32)
    if last:
        operands = (targets, prior, partners, *consts)
        out_shape = jax.ShapeDtypeStruct((peers, tb * n // peers, n * n), jnp.float32)
    else:
        operands = (targets, partners, *consts)
        out_shape = (part, part)
    return pl.pallas_call(
        functools.partial(solve_body, last, tb, nj, n),
        out_shape=out_shape,
        in_specs=[vmem] * len(operands),
        out_specs=vmem if last else (vmem, vmem),
        scratch_shapes=[
            pltpu.VMEM((4, tb * rows, quarter), jnp.bfloat16),
            pltpu.VMEM((4, tb * rows, quarter), jnp.bfloat16),
            pltpu.VMEM((tb, 2 * rows, quarter), jnp.bfloat16),
            pltpu.VMEM((4, tb * rows, quarter), jnp.float32),
        ],
        compiler_params=SOLVE_PARAMS,
        cost_estimate=pl.CostEstimate(
            flops=2 * 5 * tb * 4 * rows * quarter * quarter, bytes_accessed=8 << 20, transcendentals=0
        ),
    )(*operands)


def spread_body(copies, slab_axes, in_ref, t_ref, o_ref):
    peers, rows, plane = in_ref.shape
    each = t_ref.shape[1] // peers
    own = rows // each
    first = lax.axis_index(slab_axes) * each
    t_first = lax.axis_index("core") * own
    total = in_ref[0]
    for k in range(1, peers):
        total = total + in_ref[k]
    half = each // 2
    for core in (0, 1):
        planes = [(q, i) for q in range(half) for i in range(own)]
        picked = [total[i * each + half * core + q : i * each + half * core + q + 1] for q, i in planes]
        picked += [t_ref[t_first + i, pl.ds(first + half * core + q, 1), :] for q, i in planes]
        picked = jnp.concatenate(picked, axis=0)
        for k in range(copies):
            o_ref[2 * k + core] = picked


def spread(received, targets, copies):
    _, rows, plane = received.shape
    vmem = pl.BlockSpec(memory_space=pltpu.VMEM)
    return pl.pallas_call(
        functools.partial(spread_body, copies, SLABS),
        out_shape=jax.ShapeDtypeStruct((2 * copies, rows, plane), jnp.float32),
        in_specs=[vmem, vmem],
        out_specs=vmem,
        compiler_params=SMALL_PARAMS,
    )(received, targets)


def plane_of(ref, q, part):
    first = 8 * part + 4 * q
    return jnp.concatenate([ref[k, first : first + 4, :] for k in range(ref.shape[0])], axis=0)


def overlap_body(scale, a_ref, o_ref):
    total = None
    for q in (0, 1):
        s = lax.dot_general(
            plane_of(a_ref, q, 1),
            plane_of(a_ref, q, 0),
            (((1,), (1,)), ((), ())),
            precision=lax.Precision.HIGHEST,
            preferred_element_type=jnp.float32,
        )
        total = s if total is None else total + s
    total = total * scale
    half = total.shape[0] // 2
    packed = jnp.concatenate([total[:half], total[half:]], axis=1)
    for k in range(o_ref.shape[0]):
        o_ref[k] = packed


def overlap(slab, copies, scale):
    count = slab.shape[0] * 4
    return pl.pallas_call(
        functools.partial(overlap_body, scale),
        out_shape=jax.ShapeDtypeStruct((copies, count // 2, 2 * count), jnp.float32),
        compiler_params=SMALL_PARAMS,
    )(slab)


def compress_body(owned, s_ref, a_ref, keep_ref, o_ref, inv_ref):
    total = s_ref[0]
    for k in range(1, s_ref.shape[0]):
        total = total + s_ref[k]
    half = total.shape[0]
    count = 2 * half
    square = jnp.concatenate([total[:, :count], total[:, count:]], axis=0)
    square = 0.5 * (square + square.T)
    row = lax.broadcasted_iota(jnp.int32, (count, count), 0)
    col = lax.broadcasted_iota(jnp.int32, (count, count), 1)
    wide = jnp.concatenate([square, jnp.where(row == col, 1.0, 0.0)], axis=1)
    tiles = [wide[8 * t : 8 * t + 8] for t in range(count // 8)]
    sub = lax.broadcasted_iota(jnp.int32, (8, LANES), 0)
    down = lambda v, k: jnp.broadcast_to(v[k : k + 1], (8, LANES))
    for p in range(count // 8):
        later = range(p, count // 8)
        cols = {
            (t, k): jnp.broadcast_to(tiles[t][:, 8 * p + k : 8 * p + k + 1], (8, LANES))
            for t in later
            for k in range(8)
        }
        root = jnp.ones((8, LANES), jnp.float32)
        for k in range(8):
            pivot = down(cols[p, k], k)
            over = 1.0 / pivot
            root = jnp.where(sub == k, lax.rsqrt(pivot), root)
            line = down(tiles[p], k)
            cross = [down(cols[p, m], k) for m in range(k + 1, 8)]
            for t in later:
                f = cols[t, k] * over
                if t == p:
                    f = jnp.where(sub > k, f, 0.0)
                tiles[t] = tiles[t] - f * line
                for m in range(k + 1, 8):
                    cols[t, m] = cols[t, m] - f * cross[m - k - 1]
        inv_ref[8 * p : 8 * p + 8, :] = tiles[p] * root
    first = lax.axis_index(TGT) * owned
    mine = inv_ref[pl.ds(pl.multiple_of(first, 8), owned), :][:, count:]
    kept = first + lax.broadcasted_iota(jnp.int32, (owned, count), 0) < keep_ref[:owned, :count]
    mine = jnp.where(kept, mine, 0.0)
    for q in (0, 1):
        o_ref[:, q, :] = jnp.dot(
            mine,
            plane_of(a_ref, q, 0),
            precision=lax.Precision.HIGHEST,
            preferred_element_type=jnp.float32,
        )


def compress(summands, slab, keep, owned):
    count = slab.shape[0] * 4
    vmem = pl.BlockSpec(memory_space=pltpu.VMEM)
    return pl.pallas_call(
        functools.partial(compress_body, owned),
        out_shape=jax.ShapeDtypeStruct((owned, 2, slab.shape[2]), jnp.float32),
        in_specs=[vmem] * 3,
        out_specs=vmem,
        scratch_shapes=[pltpu.VMEM((count, LANES), jnp.float32)],
        compiler_params=SMALL_PARAMS,
    )(summands, slab, keep)


def shards(targets, partners, occupied, retained):
    owned, n, plane = targets.shape
    consts = [jnp.asarray(c) for c in tables(n, partners.shape[2] // n)]
    own_partners, keep = folded_partners(partners, occupied, retained)
    other_partners = lax.ppermute(own_partners, "core", [(0, 1), (1, 0)])
    partial_actions, folded = solve(targets, own_partners, consts)
    cut = solve(folded, other_partners, consts, partial_actions, lax.axis_size(SLABS))
    received = lax.all_to_all(cut, SLABS, 0, 0, tiled=True)
    copies = spread(received, targets, lax.axis_size(TGT))
    slab = lax.all_to_all(copies, TGT + ("core",), 0, 0, tiled=True)
    summands = overlap(slab, lax.axis_size(PTR), 1.0 / n**3)
    summands = lax.all_to_all(summands, PTR, 0, 0, tiled=True)
    return compress(summands, slab, keep, owned)


def solution(mesh):
    names = TGT + PTR
    finer = Mesh(mesh.devices.reshape(2, 4, 4, 2, 2), names)
    in_specs = (P(TGT, None, None), P(None, None, PTR), P(PTR), P())
    out_specs = P(TGT, PTR, None)
    return jax.shard_map(
        shards, mesh=finer, in_specs=in_specs, out_specs=out_specs, check_vma=False
    )
```

```python
import functools

import jax
import jax.numpy as jnp
import ml_dtypes
import numpy as np
from jax import lax
from jax.experimental import pallas as pl
from jax.experimental.pallas import tpu as pltpu
from jax.sharding import Mesh
from jax.sharding import PartitionSpec as P

TGT = ("tgt_0", "tgt_1")
PTR = ("ptr_0", "ptr_1", "core")
SLABS = ("ptr_0", "ptr_1")
LANES = 128
SOLVE_PARAMS = pltpu.CompilerParams(vmem_limit_bytes=24 << 20)
SMALL_PARAMS = pltpu.CompilerParams(vmem_limit_bytes=16 << 20)


def split_np(a):
    a = a.astype(np.float64)
    hi = a.astype(np.float32).astype(ml_dtypes.bfloat16)
    lo = (a - hi.astype(np.float64)).astype(np.float32).astype(ml_dtypes.bfloat16)
    return hi, lo


def half_bases(n):
    h = n // 2
    y = np.arange(h) + 0.5
    even_k, odd_k = np.arange(h), np.arange(1, h + 1)
    even = np.cos(2 * np.pi * even_k[:, None] * y[None] / n) * np.sqrt(2.0 / h)
    even[0] *= np.sqrt(0.5)
    odd = np.sin(2 * np.pi * odd_k[:, None] * y[None] / n) * np.sqrt(2.0 / h)
    odd[-1] *= np.sqrt(0.5)
    return (even, odd), (even_k, odd_k)


def tables(n, reps):
    bases, freqs = half_bases(n)
    planes, kernels = [], []
    ix = np.arange(n)
    wave = lambda k: (k * (2 * np.pi / n)) ** 2
    wx = wave(np.where(ix < n // 2, ix, ix - n))
    for sy in (0, 1):
        for sz in (0, 1):
            m = np.einsum("ky,lz->yzkl", bases[sy], bases[sz])
            planes.append(m.reshape(n * n // 4, n * n // 4))
            total = wx[:, None, None] + wave(freqs[sy])[:, None] + wave(freqs[sz])[None]
            g = np.where(total > 0, 4 * np.pi / np.where(total > 0, total, 1.0), 0.0)
            kernels.append(g.reshape(n, -1) / 4)
    planes = np.stack(planes)
    phase = 2 * np.pi * (ix[:, None] * ix[None] % n) / n
    wh, wl = split_np(np.kron(np.eye(reps), (np.cos(phase) + np.sin(phase)) / np.sqrt(n)))
    left = np.block([[wh, wh], [wl, np.zeros_like(wl)]]).astype(ml_dtypes.bfloat16)
    matrices = [*split_np(planes), left[None]]
    return np.concatenate(matrices), np.stack(kernels).astype(np.float32)


def split(v):
    hi = v.astype(jnp.bfloat16)
    return hi, (v - hi.astype(jnp.float32)).astype(jnp.bfloat16)


def dot(a, b):
    return jnp.dot(a, b, preferred_element_type=jnp.float32)


def dot_t(a, b):
    return lax.dot_general(a, b, (((1,), (1,)), ((), ())), preferred_element_type=jnp.float32)


def take(v, idx):
    return jnp.take_along_axis(v, idx, axis=1)


def fold(tiles, rows):
    lane = lax.broadcasted_iota(jnp.int32, (rows, LANES), 1)
    y, z = (lane // 16) % 4, lane % 16
    out = {}
    for sy in (0, 1):
        for sz in (0, 1):
            idx = (3 - y if sy else y) * 32 + (31 - z if sz else z)
            for h in (0, 1):
                a, b = (7 - 2 * h, 6 - 2 * h) if sy else (2 * h, 2 * h + 1)
                out[2 * sy + sz, h] = jnp.where(lane < 64, take(tiles[a], idx), take(tiles[b], idx))
    return out


def unfold(folded, rows):
    lane = lax.broadcasted_iota(jnp.int32, (rows, LANES), 1)
    y, z = lane // 32, lane % 32
    low = z < 16
    z = jnp.where(low, z, 31 - z)
    out = []
    for t in range(8):
        sy = t // 4
        h = (7 - t) // 2 if sy else t // 2
        first = 7 - 4 * (t % 2) if sy else 4 * (t % 2)
        idx = (first - y if sy else first + y) * 16 + z
        out.append(jnp.where(low, take(folded[2 * sy, h], idx), take(folded[2 * sy + 1, h], idx)))
    return out


def butterfly(d):
    a, b, c, e = d[0] + d[1], d[0] - d[1], d[2] + d[3], d[2] - d[3]
    return a + c, b + e, a - c, b - e


def fold_body(nj, n, p_ref, occ_hbm, keep_hbm, o_ref, keep_ref, scalars, sems):
    copies = [
        pltpu.make_async_copy(src, scalars.at[i], sems.at[i]) for i, src in enumerate((occ_hbm, keep_hbm))
    ]
    for copy in copies:
        copy.start()
    for copy in copies:
        copy.wait()
    keep_ref[...] = jnp.full(keep_ref.shape, scalars[1, 0], jnp.int32)
    occ = jnp.full((n, LANES), scalars[0, 0], jnp.int32).astype(jnp.float32)
    root = jnp.sqrt(0.25 + 0.75 * occ)
    quarter = n * n // 4
    lane = lax.broadcasted_iota(jnp.int32, (n, LANES), 1)
    for j in range(nj):
        tiles = []
        for t in range(8):
            acc = None
            for y in range(4):
                src = p_ref[pl.ds(4 * t + y, n, stride=n), :]
                if y != j:
                    src = pltpu.roll(src, ((y - j) % 4) * n, 1)
                acc = src if acc is None else jnp.where(lane // n == y, src, acc)
            tiles.append(acc * root)
        for (s, h), v in fold(tiles, n).items():
            o_ref[j * n : (j + 1) * n, s * quarter + h * LANES : s * quarter + (h + 1) * LANES] = v


def folded_partners(partners, occupied, retained):
    n = partners.shape[0]
    nj = partners.shape[2] // n
    vmem = pl.BlockSpec(memory_space=pltpu.VMEM)
    hbm = pl.BlockSpec(memory_space=pltpu.HBM)
    return pl.pallas_call(
        functools.partial(fold_body, nj, n),
        out_shape=(
            jax.ShapeDtypeStruct((nj * n, n * n), jnp.float32),
            jax.ShapeDtypeStruct((8, LANES), jnp.int32),
        ),
        in_specs=[vmem, hbm, hbm],
        out_specs=(vmem, vmem),
        scratch_shapes=[pltpu.SMEM((2, 1), jnp.int32), pltpu.SemaphoreType.DMA((2,))],
        compiler_params=SMALL_PARAMS,
        cost_estimate=pl.CostEstimate(flops=2 << 30, bytes_accessed=8 << 20, transcendentals=0),
    )(partners.reshape(n * n, -1), occupied, retained)


def solve_body(last, tb, nj, n, *refs):
    if last:
        tf, prior, pf, w_ref, k_ref, o_ref = refs[:6]
    else:
        t_ref, pf, w_ref, k_ref, o_ref, tf = refs[:6]
    gh, gl, ust, ps = refs[6:]
    rows, quarter = nj * n, n * n // 4
    if not last:
        first = lax.axis_index("core") * tb
        for i in range(tb):
            tiles = [t_ref[first + i, :, LANES * t : LANES * (t + 1)] for t in range(8)]
            for (s, h), v in fold(tiles, n).items():
                tf[i, :, s * quarter + h * LANES : s * quarter + (h + 1) * LANES] = v
    for i in range(tb):
        for j in range(nj):
            r = slice(j * n, (j + 1) * n)
            q = slice(i * rows + j * n, i * rows + (j + 1) * n)
            d = [
                tf[i, :, quarter * s : quarter * (s + 1)] * pf[r, quarter * s : quarter * (s + 1)]
                for s in range(4)
            ]
            for s, g in enumerate(butterfly(d)):
                gh[s, q, :], gl[s, q, :] = split(g)
    left = w_ref[8]
    for s in range(4):
        mh, ml = w_ref[s], w_ref[4 + s]
        u = dot(gh[s], mh) + dot(gl[s], mh) + dot(gh[s], ml)
        for i in range(tb):
            at = slice(i * rows, (i + 1) * rows)
            ust[i, :rows, :], ust[i, rows:, :] = split(u[at])
            v = dot(left, ust[i])
            v = (v[:rows] + v[rows:]).reshape(nj, n, quarter) * k_ref[s][None]
            ust[i, :rows, :], ust[i, rows:, :] = split(v.reshape(rows, quarter))
            v = dot(left, ust[i])
            gh[s, at, :], gl[s, at, :] = split(v[:rows] + v[rows:])
        ps[s] = dot_t(gh[s], mh) + dot_t(gl[s], mh) + dot_t(gh[s], ml)
    for i in range(tb):
        acc = [prior[i, :, quarter * s : quarter * (s + 1)] if last else None for s in range(4)]
        for j in range(nj):
            r = slice(j * n, (j + 1) * n)
            q = slice(i * rows + j * n, i * rows + (j + 1) * n)
            for s, v in enumerate(butterfly([ps[s, q, :] for s in range(4)])):
                v = v * pf[r, quarter * s : quarter * (s + 1)]
                acc[s] = v if acc[s] is None else acc[s] + v
        if last:
            folded = {(s, h): acc[s][:, LANES * h : LANES * (h + 1)] for s in range(4) for h in (0, 1)}
            peers = o_ref.shape[0]
            each = n // peers
            for t, v in enumerate(unfold(folded, n)):
                for d in range(peers):
                    o_ref[d, i * each : (i + 1) * each, LANES * t : LANES * (t + 1)] = v[
                        d * each : (d + 1) * each
                    ]
        else:
            for s in range(4):
                o_ref[i, :, quarter * s : quarter * (s + 1)] = acc[s]


def solve(targets, partners, consts, prior=None, peers=8):
    last = prior is not None
    n = targets.shape[1]
    nj = partners.shape[0] // n
    tb = prior.shape[0] if last else targets.shape[0] // 2
    rows, quarter = nj * n, n * n // 4
    vmem = pl.BlockSpec(memory_space=pltpu.VMEM)
    part = jax.ShapeDtypeStruct((tb, n, n * n), jnp.float32)
    if last:
        operands = (targets, prior, partners, *consts)
        out_shape = jax.ShapeDtypeStruct((peers, tb * n // peers, n * n), jnp.float32)
    else:
        operands = (targets, partners, *consts)
        out_shape = (part, part)
    return pl.pallas_call(
        functools.partial(solve_body, last, tb, nj, n),
        out_shape=out_shape,
        in_specs=[vmem] * len(operands),
        out_specs=vmem if last else (vmem, vmem),
        scratch_shapes=[
            pltpu.VMEM((4, tb * rows, quarter), jnp.bfloat16),
            pltpu.VMEM((4, tb * rows, quarter), jnp.bfloat16),
            pltpu.VMEM((tb, 2 * rows, quarter), jnp.bfloat16),
            pltpu.VMEM((4, tb * rows, quarter), jnp.float32),
        ],
        compiler_params=SOLVE_PARAMS,
        cost_estimate=pl.CostEstimate(
            flops=2 * 5 * tb * 4 * rows * quarter * quarter, bytes_accessed=8 << 20, transcendentals=0
        ),
    )(*operands)


def planes_body(slab_axes, t_ref, _, o_ref):
    each = o_ref.shape[0] // t_ref.shape[0]
    first = lax.axis_index(slab_axes) * each
    for k in range(each):
        rows = [t_ref[i, pl.ds(first + k, 1), :] for i in range(t_ref.shape[0])]
        o_ref[k * t_ref.shape[0] : (k + 1) * t_ref.shape[0], :] = jnp.concatenate(rows, axis=0)


def chip_planes(targets, after, peers):
    owned, n, plane = targets.shape
    return pl.pallas_call(
        functools.partial(planes_body, SLABS),
        out_shape=jax.ShapeDtypeStruct((owned * n // peers, plane), jnp.float32),
        compiler_params=SMALL_PARAMS,
    )(targets, after)


def total_body(in_ref, mine_ref, other_ref):
    peers, rows, _ = in_ref.shape
    total = in_ref[0]
    for k in range(1, peers):
        total = total + in_ref[k]
    own = mine_ref.shape[0] // 2
    each = rows // own
    halves = []
    for core in (0, 1):
        planes = [(q, i) for q in range(each // 2) for i in range(own)]
        picked = [total[i * each + each // 2 * core + q : i * each + each // 2 * core + q + 1] for q, i in planes]
        halves.append(jnp.concatenate(picked, axis=0))
    second = lax.axis_index("core") == 1
    mine_ref[...] = jnp.where(second, halves[1], halves[0])
    other_ref[...] = jnp.where(second, halves[0], halves[1])


def total(received):
    _, rows, plane = received.shape
    half = jax.ShapeDtypeStruct((rows // 2, plane), jnp.float32)
    return pl.pallas_call(total_body, out_shape=(half, half), compiler_params=SMALL_PARAMS)(received)


def pair_body(mine_ref, other_ref, o_ref):
    half = mine_ref.shape[0] // 2
    second = lax.axis_index("core") == 1
    mine, other = mine_ref[...], other_ref[...]
    low, high = jnp.where(second, other, mine), jnp.where(second, mine, other)
    both = [v[half * q : half * (q + 1)] for q in (0, 1) for v in (low, high)]
    both = jnp.concatenate(both, axis=0)
    for k in range(o_ref.shape[0]):
        o_ref[k] = both


def pair(mine, other, copies):
    rows, plane = mine.shape
    return pl.pallas_call(
        pair_body,
        out_shape=jax.ShapeDtypeStruct((copies, 2 * rows, plane), jnp.float32),
        compiler_params=SMALL_PARAMS,
    )(mine, other)


def plane_of(ref, q, owned=8):
    return ref[:, pl.ds(q * owned, owned), :].reshape(ref.shape[0] * owned, ref.shape[2])


def overlap_body(scale, t_ref, a_ref, o_ref):
    total = None
    first = 2 * lax.axis_index("core")
    for q in (0, 1):
        s = lax.dot_general(
            plane_of(t_ref, first + q),
            plane_of(a_ref, q),
            (((1,), (1,)), ((), ())),
            precision=lax.Precision.HIGHEST,
            preferred_element_type=jnp.float32,
        )
        total = s if total is None else total + s
    total = total * scale
    half = total.shape[0] // 2
    o_ref[...] = jnp.concatenate([total[:half], total[half:]], axis=1)


def overlap(chip_targets, slab, scale):
    count = slab.shape[0] * 8
    return pl.pallas_call(
        functools.partial(overlap_body, scale),
        out_shape=jax.ShapeDtypeStruct((count // 2, 2 * count), jnp.float32),
        compiler_params=SMALL_PARAMS,
    )(chip_targets, slab)


def repeat_body(a_ref, b_ref, o_ref):
    both = a_ref[...] + b_ref[...]
    for k in range(o_ref.shape[0]):
        o_ref[k] = both


def repeated_sum(a, b, copies):
    return pl.pallas_call(
        repeat_body,
        out_shape=jax.ShapeDtypeStruct((copies, *a.shape), jnp.float32),
        compiler_params=SMALL_PARAMS,
    )(a, b)


def compress_body(owned, s_ref, a_ref, keep_ref, o_ref, inv_ref):
    total = s_ref[0]
    for k in range(1, s_ref.shape[0]):
        total = total + s_ref[k]
    half = total.shape[0]
    count = 2 * half
    square = jnp.concatenate([total[:, :count], total[:, count:]], axis=0)
    square = 0.5 * (square + square.T)
    row = lax.broadcasted_iota(jnp.int32, (count, count), 0)
    col = lax.broadcasted_iota(jnp.int32, (count, count), 1)
    wide = jnp.concatenate([square, jnp.where(row == col, 1.0, 0.0)], axis=1)
    tiles = [wide[8 * t : 8 * t + 8] for t in range(count // 8)]
    sub = lax.broadcasted_iota(jnp.int32, (8, LANES), 0)
    down = lambda v, k: jnp.broadcast_to(v[k : k + 1], (8, LANES))
    for p in range(count // 8):
        later = range(p, count // 8)
        cols = {
            (t, k): jnp.broadcast_to(tiles[t][:, 8 * p + k : 8 * p + k + 1], (8, LANES))
            for t in later
            for k in range(8)
        }
        root = jnp.ones((8, LANES), jnp.float32)
        for k in range(8):
            pivot = down(cols[p, k], k)
            over = 1.0 / pivot
            root = jnp.where(sub == k, lax.rsqrt(pivot), root)
            line = down(tiles[p], k)
            cross = [down(cols[p, m], k) for m in range(k + 1, 8)]
            for t in later:
                f = cols[t, k] * over
                if t == p:
                    f = jnp.where(sub > k, f, 0.0)
                tiles[t] = tiles[t] - f * line
                for m in range(k + 1, 8):
                    cols[t, m] = cols[t, m] - f * cross[m - k - 1]
        inv_ref[8 * p : 8 * p + 8, :] = tiles[p] * root
    first = lax.axis_index(TGT) * owned
    mine = inv_ref[pl.ds(pl.multiple_of(first, 8), owned), :][:, count:]
    kept = first + lax.broadcasted_iota(jnp.int32, (owned, count), 0) < keep_ref[:owned, :count]
    mine = jnp.where(kept, mine, 0.0)
    for q in (0, 1):
        o_ref[:, q, :] = jnp.dot(
            mine,
            plane_of(a_ref, q),
            precision=lax.Precision.HIGHEST,
            preferred_element_type=jnp.float32,
        )


def compress(summands, slab, keep, owned):
    count = slab.shape[0] * owned
    vmem = pl.BlockSpec(memory_space=pltpu.VMEM)
    return pl.pallas_call(
        functools.partial(compress_body, owned),
        out_shape=jax.ShapeDtypeStruct((owned, 2, slab.shape[2]), jnp.float32),
        in_specs=[vmem] * 3,
        out_specs=vmem,
        scratch_shapes=[pltpu.VMEM((count, LANES), jnp.float32)],
        compiler_params=SMALL_PARAMS,
    )(summands, slab, keep)


def shards(targets, partners, occupied, retained):
    owned, n, plane = targets.shape
    consts = [jnp.asarray(c) for c in tables(n, partners.shape[2] // n)]
    peers, groups = lax.axis_size(SLABS), lax.axis_size(TGT)
    swap = [(0, 1), (1, 0)]
    own_partners, keep = folded_partners(partners, occupied, retained)
    other_partners = lax.ppermute(own_partners, "core", swap)
    chip_targets = lax.all_gather(chip_planes(targets, keep, peers), TGT, axis=0)
    partial_actions, folded = solve(targets, own_partners, consts)
    cut = solve(folded, other_partners, consts, partial_actions, peers)
    mine, other = total(lax.all_to_all(cut, SLABS, 0, 0, tiled=True))
    slab = lax.all_to_all(pair(mine, lax.ppermute(other, "core", swap), groups), TGT, 0, 0, tiled=True)
    part = overlap(chip_targets, slab, 1.0 / n**3)
    summands = repeated_sum(part, lax.ppermute(part, "core", swap), peers)
    summands = lax.all_to_all(summands, SLABS, 0, 0, tiled=True)
    return compress(summands, slab, keep, owned)


def solution(mesh):
    names = TGT + PTR
    finer = Mesh(mesh.devices.reshape(2, 4, 4, 2, 2), names)
    in_specs = (P(TGT, None, None), P(None, None, PTR), P(PTR), P())
    out_specs = P(TGT, PTR, None)
    return jax.shard_map(
        shards, mesh=finer, in_specs=in_specs, out_specs=out_specs, check_vma=False
    )
```

```python
import functools

import jax
import jax.numpy as jnp
import ml_dtypes
import numpy as np
from jax import lax
from jax.experimental import pallas as pl
from jax.experimental.pallas import tpu as pltpu
from jax.sharding import Mesh
from jax.sharding import PartitionSpec as P

TGT = ("tgt_0", "tgt_1")
PTR = ("ptr_0", "ptr_1", "core")
LANES = 128
SOLVE_PARAMS = pltpu.CompilerParams(vmem_limit_bytes=24 << 20)
SMALL_PARAMS = pltpu.CompilerParams(vmem_limit_bytes=16 << 20)


def split_np(a):
    a = a.astype(np.float64)
    hi = a.astype(np.float32).astype(ml_dtypes.bfloat16)
    lo = (a - hi.astype(np.float64)).astype(np.float32).astype(ml_dtypes.bfloat16)
    return hi, lo


def half_bases(n):
    h = n // 2
    y = np.arange(h) + 0.5
    even_k, odd_k = np.arange(h), np.arange(1, h + 1)
    even = np.cos(2 * np.pi * even_k[:, None] * y[None] / n) * np.sqrt(2.0 / h)
    even[0] *= np.sqrt(0.5)
    odd = np.sin(2 * np.pi * odd_k[:, None] * y[None] / n) * np.sqrt(2.0 / h)
    odd[-1] *= np.sqrt(0.5)
    return (even, odd), (even_k, odd_k)


def tables(n, reps):
    bases, freqs = half_bases(n)
    planes, kernels = [], []
    ix = np.arange(n)
    wave = lambda k: (k * (2 * np.pi / n)) ** 2
    wx = wave(np.where(ix < n // 2, ix, ix - n))
    for sy in (0, 1):
        for sz in (0, 1):
            m = np.einsum("ky,lz->yzkl", bases[sy], bases[sz])
            planes.append(m.reshape(n * n // 4, n * n // 4))
            total = wx[:, None, None] + wave(freqs[sy])[:, None] + wave(freqs[sz])[None]
            g = np.where(total > 0, 4 * np.pi / np.where(total > 0, total, 1.0), 0.0)
            kernels.append(g.reshape(n, -1) / 4)
    planes = np.stack(planes)
    phase = 2 * np.pi * (ix[:, None] * ix[None] % n) / n
    wh, wl = split_np(np.kron(np.eye(reps), (np.cos(phase) + np.sin(phase)) / np.sqrt(n)))
    left = np.block([[wh, wh], [wl, np.zeros_like(wl)]]).astype(ml_dtypes.bfloat16)
    matrices = [*split_np(planes), left[None]]
    return np.concatenate(matrices), np.stack(kernels).astype(np.float32)


def split(v):
    hi = v.astype(jnp.bfloat16)
    return hi, (v - hi.astype(jnp.float32)).astype(jnp.bfloat16)


def dot(a, b):
    return jnp.dot(a, b, preferred_element_type=jnp.float32)


def dot_t(a, b):
    return lax.dot_general(a, b, (((1,), (1,)), ((), ())), preferred_element_type=jnp.float32)


def take(v, idx):
    return jnp.take_along_axis(v, idx, axis=1)


def fold(tiles, rows):
    lane = lax.broadcasted_iota(jnp.int32, (rows, LANES), 1)
    y, z = (lane // 16) % 4, lane % 16
    out = {}
    for sy in (0, 1):
        for sz in (0, 1):
            idx = (3 - y if sy else y) * 32 + (31 - z if sz else z)
            for h in (0, 1):
                a, b = (7 - 2 * h, 6 - 2 * h) if sy else (2 * h, 2 * h + 1)
                out[2 * sy + sz, h] = jnp.where(lane < 64, take(tiles[a], idx), take(tiles[b], idx))
    return out


def unfold(folded, rows):
    lane = lax.broadcasted_iota(jnp.int32, (rows, LANES), 1)
    y, z = lane // 32, lane % 32
    low = z < 16
    z = jnp.where(low, z, 31 - z)
    out = []
    for t in range(8):
        sy = t // 4
        h = (7 - t) // 2 if sy else t // 2
        first = 7 - 4 * (t % 2) if sy else 4 * (t % 2)
        idx = (first - y if sy else first + y) * 16 + z
        out.append(jnp.where(low, take(folded[2 * sy, h], idx), take(folded[2 * sy + 1, h], idx)))
    return out


def butterfly(d):
    a, b, c, e = d[0] + d[1], d[0] - d[1], d[2] + d[3], d[2] - d[3]
    return a + c, b + e, a - c, b - e


def fold_body(nj, n, p_ref, occ_hbm, keep_hbm, o_ref, keep_ref, scalars, sems):
    copies = [
        pltpu.make_async_copy(src, scalars.at[i], sems.at[i]) for i, src in enumerate((occ_hbm, keep_hbm))
    ]
    for copy in copies:
        copy.start()
    for copy in copies:
        copy.wait()
    keep_ref[...] = jnp.full(keep_ref.shape, scalars[1, 0], jnp.int32)
    occ = jnp.full((n, LANES), scalars[0, 0], jnp.int32).astype(jnp.float32)
    root = jnp.sqrt(0.25 + 0.75 * occ)
    quarter = n * n // 4
    lane = lax.broadcasted_iota(jnp.int32, (n, LANES), 1)
    for j in range(nj):
        tiles = []
        for t in range(8):
            acc = None
            for y in range(4):
                src = p_ref[pl.ds(4 * t + y, n, stride=n), :]
                if y != j:
                    src = pltpu.roll(src, ((y - j) % 4) * n, 1)
                acc = src if acc is None else jnp.where(lane // n == y, src, acc)
            tiles.append(acc * root)
        for (s, h), v in fold(tiles, n).items():
            o_ref[j * n : (j + 1) * n, s * quarter + h * LANES : s * quarter + (h + 1) * LANES] = v


def folded_partners(partners, occupied, retained):
    n = partners.shape[0]
    nj = partners.shape[2] // n
    vmem = pl.BlockSpec(memory_space=pltpu.VMEM)
    hbm = pl.BlockSpec(memory_space=pltpu.HBM)
    return pl.pallas_call(
        functools.partial(fold_body, nj, n),
        out_shape=(
            jax.ShapeDtypeStruct((nj * n, n * n), jnp.float32),
            jax.ShapeDtypeStruct((8, LANES), jnp.int32),
        ),
        in_specs=[vmem, hbm, hbm],
        out_specs=(vmem, vmem),
        scratch_shapes=[pltpu.SMEM((2, 1), jnp.int32), pltpu.SemaphoreType.DMA((2,))],
        compiler_params=SMALL_PARAMS,
        cost_estimate=pl.CostEstimate(flops=2 << 30, bytes_accessed=8 << 20, transcendentals=0),
    )(partners.reshape(n * n, -1), occupied, retained)


def solve_body(last, tb, nj, n, *refs):
    if last:
        tf, prior, pf, w_ref, k_ref, o_ref = refs[:6]
    else:
        t_ref, pf, w_ref, k_ref, o_ref, tf = refs[:6]
    gh, gl, ust, ps = refs[-4:]
    rows, quarter = nj * n, n * n // 4
    if not last:
        first = lax.axis_index("core") * tb
        for i in range(tb):
            tiles = [t_ref[first + i, :, LANES * t : LANES * (t + 1)] for t in range(8)]
            for (s, h), v in fold(tiles, n).items():
                tf[i, :, s * quarter + h * LANES : s * quarter + (h + 1) * LANES] = v
    for i in range(tb):
        for j in range(nj):
            r = slice(j * n, (j + 1) * n)
            q = slice(i * rows + j * n, i * rows + (j + 1) * n)
            d = [
                tf[i, :, quarter * s : quarter * (s + 1)] * pf[r, quarter * s : quarter * (s + 1)]
                for s in range(4)
            ]
            for s, g in enumerate(butterfly(d)):
                gh[s, q, :], gl[s, q, :] = split(g)
    left = w_ref[8]
    for s in range(4):
        mh, ml = w_ref[s], w_ref[4 + s]
        u = dot(gh[s], mh) + dot(gl[s], mh) + dot(gh[s], ml)
        for i in range(tb):
            at = slice(i * rows, (i + 1) * rows)
            ust[i, :rows, :], ust[i, rows:, :] = split(u[at])
            v = dot(left, ust[i])
            v = (v[:rows] + v[rows:]).reshape(nj, n, quarter) * k_ref[s][None]
            ust[i, :rows, :], ust[i, rows:, :] = split(v.reshape(rows, quarter))
            v = dot(left, ust[i])
            gh[s, at, :], gl[s, at, :] = split(v[:rows] + v[rows:])
        ps[s] = dot_t(gh[s], mh) + dot_t(gl[s], mh) + dot_t(gh[s], ml)
    for i in range(tb):
        acc = [prior[i, :, quarter * s : quarter * (s + 1)] if last else None for s in range(4)]
        for j in range(nj):
            r = slice(j * n, (j + 1) * n)
            q = slice(i * rows + j * n, i * rows + (j + 1) * n)
            for s, v in enumerate(butterfly([ps[s, q, :] for s in range(4)])):
                v = v * pf[r, quarter * s : quarter * (s + 1)]
                acc[s] = v if acc[s] is None else acc[s] + v
        if last:
            folded = {(s, h): acc[s][:, LANES * h : LANES * (h + 1)] for s in range(4) for h in (0, 1)}
            peers = o_ref.shape[0]
            each = n // peers
            for t, v in enumerate(unfold(folded, n)):
                for d in range(peers):
                    o_ref[d, i * each : (i + 1) * each, LANES * t : LANES * (t + 1)] = v[
                        d * each : (d + 1) * each
                    ]
        else:
            for s in range(4):
                o_ref[i, :, quarter * s : quarter * (s + 1)] = acc[s]


def solve(targets, partners, consts, prior=None, peers=16):
    last = prior is not None
    n = targets.shape[1]
    nj = partners.shape[0] // n
    tb = prior.shape[0] if last else targets.shape[0] // 2
    rows, quarter = nj * n, n * n // 4
    vmem = pl.BlockSpec(memory_space=pltpu.VMEM)
    part = jax.ShapeDtypeStruct((tb, n, n * n), jnp.float32)
    if last:
        operands = (targets, prior, partners, *consts)
        out_shape = jax.ShapeDtypeStruct((peers, tb * n // peers, n * n), jnp.float32)
    else:
        operands = (targets, partners, *consts)
        out_shape = (part, part)
    return pl.pallas_call(
        functools.partial(solve_body, last, tb, nj, n),
        out_shape=out_shape,
        in_specs=[vmem] * len(operands),
        out_specs=vmem if last else (vmem, vmem),
        scratch_shapes=[
            pltpu.VMEM((4, tb * rows, quarter), jnp.bfloat16),
            pltpu.VMEM((4, tb * rows, quarter), jnp.bfloat16),
            pltpu.VMEM((tb, 2 * rows, quarter), jnp.bfloat16),
            pltpu.VMEM((4, tb * rows, quarter), jnp.float32),
        ],
        compiler_params=SOLVE_PARAMS,
        cost_estimate=pl.CostEstimate(
            flops=2 * 5 * tb * 4 * rows * quarter * quarter, bytes_accessed=8 << 20, transcendentals=0
        ),
    )(*operands)


def spread_body(in_ref, o_ref):
    peers, rows, _ = in_ref.shape
    halves = []
    for core in (0, 1):
        total = in_ref[core]
        for k in range(core + 2, peers, 2):
            total = total + in_ref[k]
        halves.append(total)
    order = [v[2 * i + q : 2 * i + q + 1] for q in (0, 1) for v in halves for i in range(rows // 2)]
    slab = jnp.concatenate(order, axis=0)
    for k in range(o_ref.shape[0]):
        o_ref[k] = slab


def spread(received, copies):
    _, rows, plane = received.shape
    return pl.pallas_call(
        spread_body,
        out_shape=jax.ShapeDtypeStruct((copies, 2 * rows, plane), jnp.float32),
        compiler_params=SMALL_PARAMS,
    )(received)


def plane_of(ref, q):
    half = ref.shape[1] // 2
    return ref[:, q * half : (q + 1) * half, :].reshape(ref.shape[0] * half, ref.shape[2])


def overlap_body(scale, t_ref, a_ref, o_ref):
    owned = t_ref.shape[0]
    first = 2 * lax.axis_index(PTR)
    total = None
    for q in (0, 1):
        t = [t_ref[i, pl.ds(first + q, 1), :] for i in range(owned)]
        s = lax.dot_general(
            jnp.concatenate(t, axis=0),
            plane_of(a_ref, q),
            (((1,), (1,)), ((), ())),
            precision=lax.Precision.HIGHEST,
            preferred_element_type=jnp.float32,
        )
        total = s if total is None else total + s
    total = total * scale
    packed = jnp.concatenate([total[: owned // 2], total[owned // 2 :]], axis=1)
    for k in range(o_ref.shape[0]):
        o_ref[k] = packed


def overlap(targets, slab, copies, scale):
    owned = targets.shape[0]
    count = slab.shape[0] * owned
    return pl.pallas_call(
        functools.partial(overlap_body, scale),
        out_shape=jax.ShapeDtypeStruct((copies, owned // 2, 2 * count), jnp.float32),
        compiler_params=SMALL_PARAMS,
    )(targets, slab)


def compress_body(owned, s_ref, a_ref, keep_ref, o_ref, inv_ref):
    groups = lax.axis_size(TGT)
    slabs = s_ref.shape[0] // groups
    count = groups * owned
    rows = []
    for t in range(groups):
        total = s_ref[t * slabs]
        for k in range(1, slabs):
            total = total + s_ref[t * slabs + k]
        rows += [total[:, :count], total[:, count:]]
    square = jnp.concatenate(rows, axis=0)
    square = 0.5 * (square + square.T)
    row = lax.broadcasted_iota(jnp.int32, (count, count), 0)
    col = lax.broadcasted_iota(jnp.int32, (count, count), 1)
    wide = jnp.concatenate([square, jnp.where(row == col, 1.0, 0.0)], axis=1)
    tiles = [wide[8 * t : 8 * t + 8] for t in range(count // 8)]
    sub = lax.broadcasted_iota(jnp.int32, (8, LANES), 0)
    down = lambda v, k: jnp.broadcast_to(v[k : k + 1], (8, LANES))
    for p in range(count // 8):
        later = range(p, count // 8)
        cols = {
            (t, k): jnp.broadcast_to(tiles[t][:, 8 * p + k : 8 * p + k + 1], (8, LANES))
            for t in later
            for k in range(8)
        }
        root = jnp.ones((8, LANES), jnp.float32)
        for k in range(8):
            pivot = down(cols[p, k], k)
            over = 1.0 / pivot
            root = jnp.where(sub == k, lax.rsqrt(pivot), root)
            line = down(tiles[p], k)
            cross = [down(cols[p, m], k) for m in range(k + 1, 8)]
            for t in later:
                f = cols[t, k] * over
                if t == p:
                    f = jnp.where(sub > k, f, 0.0)
                tiles[t] = tiles[t] - f * line
                for m in range(k + 1, 8):
                    cols[t, m] = cols[t, m] - f * cross[m - k - 1]
        inv_ref[8 * p : 8 * p + 8, :] = tiles[p] * root
    first = lax.axis_index(TGT) * owned
    mine = inv_ref[pl.ds(pl.multiple_of(first, 8), owned), :][:, count:]
    kept = first + lax.broadcasted_iota(jnp.int32, (owned, count), 0) < keep_ref[:owned, :count]
    mine = jnp.where(kept, mine, 0.0)
    for q in (0, 1):
        o_ref[:, q, :] = jnp.dot(
            mine,
            plane_of(a_ref, q),
            precision=lax.Precision.HIGHEST,
            preferred_element_type=jnp.float32,
        )


def compress(summands, slab, keep, owned):
    count = slab.shape[0] * owned
    vmem = pl.BlockSpec(memory_space=pltpu.VMEM)
    return pl.pallas_call(
        functools.partial(compress_body, owned),
        out_shape=jax.ShapeDtypeStruct((owned, 2, slab.shape[2]), jnp.float32),
        in_specs=[vmem] * 3,
        out_specs=vmem,
        scratch_shapes=[pltpu.VMEM((count, LANES), jnp.float32)],
        compiler_params=SMALL_PARAMS,
    )(summands, slab, keep)


def shards(targets, partners, occupied, retained):
    owned, n, plane = targets.shape
    consts = [jnp.asarray(c) for c in tables(n, partners.shape[2] // n)]
    peers, groups = lax.axis_size(PTR), lax.axis_size(TGT)
    swap = [(0, 1), (1, 0)]
    own_partners, keep = folded_partners(partners, occupied, retained)
    other_partners = lax.ppermute(own_partners, "core", swap)
    partial_actions, folded = solve(targets, own_partners, consts)
    cut = solve(folded, other_partners, consts, partial_actions, peers)
    copies = spread(lax.all_to_all(cut, PTR, 0, 0, tiled=True), groups)
    slab = lax.all_to_all(copies, TGT, 0, 0, tiled=True)
    summands = overlap(targets, slab, lax.axis_size(TGT + PTR), 1.0 / n**3)
    summands = lax.all_to_all(summands, TGT + PTR, 0, 0, tiled=True)
    return compress(summands, slab, keep, owned)


def solution(mesh):
    names = TGT + PTR
    finer = Mesh(mesh.devices.reshape(2, 4, 4, 2, 2), names)
    in_specs = (P(TGT, None, None), P(None, None, PTR), P(PTR), P())
    out_specs = P(TGT, PTR, None)
    return jax.shard_map(
        shards, mesh=finer, in_specs=in_specs, out_specs=out_specs, check_vma=False
    )
```

```python
import functools

import jax
import jax.numpy as jnp
import ml_dtypes
import numpy as np
from jax import lax
from jax.experimental import pallas as pl
from jax.experimental.pallas import tpu as pltpu
from jax.sharding import Mesh
from jax.sharding import PartitionSpec as P

TGT = ("tgt_0", "tgt_1")
PTR = ("ptr_0", "ptr_1", "core")
LANES = 128
SOLVE_PARAMS = pltpu.CompilerParams(vmem_limit_bytes=24 << 20)
SMALL_PARAMS = pltpu.CompilerParams(vmem_limit_bytes=16 << 20)


def split_np(a):
    a = a.astype(np.float64)
    hi = a.astype(np.float32).astype(ml_dtypes.bfloat16)
    lo = (a - hi.astype(np.float64)).astype(np.float32).astype(ml_dtypes.bfloat16)
    return hi, lo


def half_bases(n):
    h = n // 2
    y = np.arange(h) + 0.5
    even_k, odd_k = np.arange(h), np.arange(1, h + 1)
    even = np.cos(2 * np.pi * even_k[:, None] * y[None] / n) * np.sqrt(2.0 / h)
    even[0] *= np.sqrt(0.5)
    odd = np.sin(2 * np.pi * odd_k[:, None] * y[None] / n) * np.sqrt(2.0 / h)
    odd[-1] *= np.sqrt(0.5)
    return (even, odd), (even_k, odd_k)


def tables(n):
    bases, freqs = half_bases(n)
    half = n // 2
    planes, kernels = [], []
    wave = lambda k: (k * (2 * np.pi / n)) ** 2
    ix = np.arange(half)
    weight = np.where(ix == 0, 1.0, 2.0) / half / 8
    for sy in (0, 1):
        for sz in (0, 1):
            m = np.einsum("ky,lz->yzkl", bases[sy], bases[sz])
            planes.append(m.reshape(half * half, half * half))
            for wx in (wave(ix), wave(half - ix)):
                total = wx[:, None, None] + wave(freqs[sy])[:, None] + wave(freqs[sz])[None]
                g = np.where(total > 0, 4 * np.pi / np.where(total > 0, total, 1.0), 0.0)
                kernels.append((g * weight[:, None, None]).reshape(half, -1, LANES))
    kernels = np.stack(kernels).reshape(4, n, -1, LANES).transpose(0, 2, 1, 3)
    return np.concatenate(split_np(np.stack(planes))), kernels.reshape(-1, n, LANES).astype(np.float32)


def split(v):
    hi = v.astype(jnp.bfloat16)
    return hi, (v - hi.astype(jnp.float32)).astype(jnp.bfloat16)


def dot(a, b):
    return jnp.dot(a, b, preferred_element_type=jnp.float32)


def dot_t(a, b):
    return lax.dot_general(a, b, (((1,), (1,)), ((), ())), preferred_element_type=jnp.float32)


def take(v, idx):
    return jnp.take_along_axis(v, idx, axis=1)


def fold(tiles, rows):
    lane = lax.broadcasted_iota(jnp.int32, (rows, LANES), 1)
    y, z = (lane // 16) % 4, lane % 16
    out = {}
    for sy in (0, 1):
        for sz in (0, 1):
            idx = (3 - y if sy else y) * 32 + (31 - z if sz else z)
            for h in (0, 1):
                a, b = (7 - 2 * h, 6 - 2 * h) if sy else (2 * h, 2 * h + 1)
                out[2 * sy + sz, h] = jnp.where(lane < 64, take(tiles[a], idx), take(tiles[b], idx))
    return out


def unfold(folded, rows):
    lane = lax.broadcasted_iota(jnp.int32, (rows, LANES), 1)
    y, z = lane // 32, lane % 32
    low = z < 16
    z = jnp.where(low, z, 31 - z)
    out = []
    for t in range(8):
        sy = t // 4
        h = (7 - t) // 2 if sy else t // 2
        first = 7 - 4 * (t % 2) if sy else 4 * (t % 2)
        idx = (first - y if sy else first + y) * 16 + z
        out.append(jnp.where(low, take(folded[2 * sy, h], idx), take(folded[2 * sy + 1, h], idx)))
    return out


def cosines(v):
    n = len(v)
    if n == 1:
        return v
    half = n // 2
    even = cosines([v[i] + v[n - 1 - i] for i in range(half)])
    if n == 2:
        return [even[0], (v[0] - v[1]) * np.float32(np.sqrt(0.5))]
    scale = [np.float32(2 * np.cos(np.pi * (2 * i + 1) / (2 * n))) for i in range(half)]
    odd = cosines([(v[i] - v[n - 1 - i]) * scale[i] for i in range(half)])
    out = [even[0], odd[0] * np.float32(0.5)]
    for k in range(1, half):
        out += [even[k], odd[k] - out[-1]]
    return out


def cosines_t(x):
    n = len(x)
    if n == 1:
        return x
    half = n // 2
    even = cosines_t(x[0::2])
    if n == 2:
        b = [x[1] * np.float32(np.sqrt(0.5))]
    else:
        z = [x[n - 1]]
        for k in range(half - 2, -1, -1):
            z.insert(0, x[2 * k + 1] - z[0])
        z[0] = z[0] * np.float32(0.5)
        scale = [np.float32(2 * np.cos(np.pi * (2 * i + 1) / (2 * n))) for i in range(half)]
        b = [c * w for c, w in zip(cosines_t(z), scale)]
    return [even[i] + b[i] for i in range(half)] + [even[i] - b[i] for i in range(half - 1, -1, -1)]


def along_x(v, table):
    half = len(v) // 2
    even = [v[i] + v[-1 - i] for i in range(half)]
    odd = [v[-1 - i] - v[i] if i % 2 else v[i] - v[-1 - i] for i in range(half)]
    even = cosines_t([c * table(k) for k, c in enumerate(cosines(even))])
    odd = cosines_t([c * table(half + k) for k, c in enumerate(cosines(odd))])
    low = [e - o if i % 2 else e + o for i, (e, o) in enumerate(zip(even, odd))]
    high = [e + o if i % 2 else e - o for i, (e, o) in enumerate(zip(even, odd))]
    return low + high[::-1]


def butterfly(d):
    a, b, c, e = d[0] + d[1], d[0] - d[1], d[2] + d[3], d[2] - d[3]
    return a + c, b + e, a - c, b - e


def fold_body(nj, n, p_ref, occ_ref, rank_ref, o_ref, keep_ref):
    keep_ref[...] = jnp.full(keep_ref.shape, rank_ref[0], jnp.int32)
    occ = jnp.full((n, LANES), occ_ref[0], jnp.int32).astype(jnp.float32)
    root = jnp.sqrt(0.25 + 0.75 * occ)
    lane = lax.broadcasted_iota(jnp.int32, (n, LANES), 1)
    part = lane // n
    tiles = [[] for _ in range(nj)]
    for t in range(n // nj):
        src = [p_ref[pl.ds(nj * t + y, n, stride=n), :] * root for y in range(nj)]
        for j in range(nj):
            acc = src[j]
            for y in range(nj):
                if y != j:
                    acc = jnp.where(part == y, pltpu.roll(src[y], ((y - j) % nj) * n, 1), acc)
            tiles[j].append(acc)
    for j in range(nj):
        for (s, h), v in fold(tiles[j], n).items():
            o_ref[2 * s + h, j * n : (j + 1) * n, :] = v


def folded_partners(partners, occupied, retained):
    n = partners.shape[0]
    nj = partners.shape[2] // n
    vmem = pl.BlockSpec(memory_space=pltpu.VMEM)
    smem = pl.BlockSpec(memory_space=pltpu.SMEM)
    return pl.pallas_call(
        functools.partial(fold_body, nj, n),
        out_shape=(
            jax.ShapeDtypeStruct((n * n // LANES, nj * n, LANES), jnp.float32),
            jax.ShapeDtypeStruct((8, LANES), jnp.int32),
        ),
        in_specs=[vmem, smem, smem],
        out_specs=(vmem, vmem),
        compiler_params=SMALL_PARAMS,
        cost_estimate=pl.CostEstimate(flops=2 << 30, bytes_accessed=8 << 20, transcendentals=0),
    )(partners.reshape(n * n, -1), occupied, retained)


def solve_body(last, tb, n, *refs):
    if last:
        t8, prior, p_ref, w_ref, k_ref, o_ref, p8, gh, gl, ps = refs
    else:
        t_ref, p_ref, w_ref, k_ref, o_ref, t8, p8, gh, gl, ps, rows_ref = refs
    quarter = n * n // 4
    tiles = n * n // LANES
    pairs = p8.shape[0]
    sub = lax.broadcasted_iota(jnp.int32, (8, LANES), 0)
    upper, second, late = sub < tb, sub % 2 == 1, sub % tb >= 2
    at = lambda k: slice(LANES * k, LANES * (k + 1))
    cls = lambda s: slice(quarter * s, quarter * (s + 1))
    if not last:
        first = lax.axis_index("core") * tb
        for i in range(tb):
            folded = fold([t_ref[first + i, :, at(k)] for k in range(tiles)], n)
            for (s, h), v in folded.items():
                rows_ref[2 * s + h, i * n : (i + 1) * n, :] = v
        for k in range(tiles):
            for x in range(n):
                rows = [rows_ref[k, pl.ds(i * n + x, 8, stride=0), :] for i in range(tb)]
                low, high = jnp.where(second, rows[1], rows[0]), jnp.where(second, rows[3], rows[2])
                t8[x, :, at(k)] = jnp.where(late, high, low)
    for g in range(pairs):
        for k in range(tiles):
            for x in range(n):
                a, b = (
                    p_ref[k, pl.ds(j * n + x, 8, stride=0), :] for j in (2 * g, 2 * g + 1)
                )
                p8[g, x, :, at(k)] = jnp.where(upper, a, b)
    for g in range(pairs):
        for x in range(0, n, 2):
            both = []
            for y in (x, x + 1):
                both.append(butterfly([t8[y, :, cls(s)] * p8[g, y, :, cls(s)] for s in range(4)]))
            q = slice((g * n + x) * 8, (g * n + x + 2) * 8)
            for s in range(4):
                gh[s, q, :], gl[s, q, :] = split(jnp.concatenate([both[0][s], both[1][s]], axis=0))

    def forward(s):
        ps[s] = dot(gh[s], w_ref[s]) + dot(gl[s], w_ref[s]) + dot(gh[s], w_ref[4 + s])

    def middle(s):
        for g in range(pairs):
            for h in range(quarter // LANES):
                v = [ps[s, (g * n + x) * 8 : (g * n + x + 1) * 8, at(h)] for x in range(n)]
                k = s * (quarter // LANES) + h
                v = along_x(v, lambda r, k=k: k_ref[k, pl.ds(r, 8, stride=0), :])
                for x in range(0, n, 2):
                    q = slice((g * n + x) * 8, (g * n + x + 2) * 8)
                    gh[s, q, at(h)], gl[s, q, at(h)] = split(jnp.concatenate(v[x : x + 2], axis=0))

    def back(s):
        ps[s] = dot_t(gh[s], w_ref[s]) + dot_t(gl[s], w_ref[s]) + dot_t(gh[s], w_ref[4 + s])

    forward(0)
    forward(1)
    middle(0)
    forward(2)
    middle(1)
    back(0)
    forward(3)
    middle(2)
    back(1)
    middle(3)
    back(2)
    back(3)
    done = []
    for x in range(n):
        acc = [prior[x, :, cls(s)] if last else None for s in range(4)]
        for g in range(pairs):
            q = slice((g * n + x) * 8, (g * n + x + 1) * 8)
            for s, v in enumerate(butterfly([ps[s, q, :] for s in range(4)])):
                v = v * p8[g, x, :, cls(s)]
                acc[s] = v if acc[s] is None else acc[s] + v
        if not last:
            for s in range(4):
                o_ref[x, :, cls(s)] = acc[s]
            continue
        done.append(acc)
        if len(done) == 2:
            folded = {}
            for s in range(4):
                for h in range(quarter // LANES):
                    a, b = (v[s][:, at(h)] for v in done)
                    folded[s, h] = jnp.where(upper, a, pltpu.roll(b, tb, 0)) + jnp.where(upper, pltpu.roll(a, tb, 0), b)
            for k, v in enumerate(unfold(folded, 8)):
                o_ref[x // 2, :, at(k)] = v
            done = []


def solve(targets, partners, consts, prior=None):
    last = prior is not None
    tiles, rows, _ = partners.shape
    n, tb = 32, 4
    pairs = rows // n // 2
    vmem = pl.BlockSpec(memory_space=pltpu.VMEM)
    part = jax.ShapeDtypeStruct((n, 2 * tb, n * n), jnp.float32)
    if last:
        operands = (targets, prior, partners, *consts)
        out_shape = jax.ShapeDtypeStruct((n // 2, 2 * tb, n * n), jnp.float32)
    else:
        operands = (targets, partners, *consts)
        out_shape = (part, part)
    long = pairs * n * 2 * tb
    scratch = [
        pltpu.VMEM((pairs, n, 2 * tb, n * n), jnp.float32),
        pltpu.VMEM((4, long, n * n // 4), jnp.bfloat16),
        pltpu.VMEM((4, long, n * n // 4), jnp.bfloat16),
        pltpu.VMEM((4, long, n * n // 4), jnp.float32),
    ]
    if not last:
        scratch.append(pltpu.VMEM((tiles, tb * n, LANES), jnp.float32))
    return pl.pallas_call(
        functools.partial(solve_body, last, tb, n),
        out_shape=out_shape,
        in_specs=[vmem] * len(operands),
        out_specs=vmem if last else (vmem, vmem),
        scratch_shapes=scratch,
        compiler_params=SOLVE_PARAMS,
        cost_estimate=pl.CostEstimate(
            flops=2 * 6 * long * (n * n // 2) ** 2, bytes_accessed=8 << 20, transcendentals=0
        ),
    )(*operands)


def spread_body(in_ref, o_ref):
    peers, rows, _ = in_ref.shape
    halves = []
    for core in (0, 1):
        total = in_ref[core]
        for k in range(core + 2, peers, 2):
            total = total + in_ref[k]
        halves.append(total)
    order = [v[q * rows // 2 : (q + 1) * rows // 2] for q in (0, 1) for v in halves]
    slab = jnp.concatenate(order, axis=0)
    for k in range(o_ref.shape[0]):
        o_ref[k] = slab


def spread(received, copies):
    _, rows, plane = received.shape
    return pl.pallas_call(
        spread_body,
        out_shape=jax.ShapeDtypeStruct((copies, 2 * rows, plane), jnp.float32),
        compiler_params=SMALL_PARAMS,
    )(received)


def plane_of(ref, q):
    half = ref.shape[1] // 2
    return ref[:, q * half : (q + 1) * half, :].reshape(ref.shape[0] * half, ref.shape[2])


def overlap_body(scale, t_ref, a_ref, o_ref):
    owned = t_ref.shape[0]
    first = 2 * lax.axis_index(PTR)
    total = None
    for q in (0, 1):
        t = [t_ref[i, pl.ds(first + q, 1), :] for i in range(owned)]
        s = lax.dot_general(
            jnp.concatenate(t, axis=0),
            plane_of(a_ref, q),
            (((1,), (1,)), ((), ())),
            precision=lax.Precision.HIGHEST,
            preferred_element_type=jnp.float32,
        )
        total = s if total is None else total + s
    total = total * scale
    packed = jnp.concatenate([total[: owned // 2], total[owned // 2 :]], axis=1)
    for k in range(o_ref.shape[0]):
        o_ref[k] = packed


def overlap(targets, slab, copies, scale):
    owned = targets.shape[0]
    count = slab.shape[0] * owned
    return pl.pallas_call(
        functools.partial(overlap_body, scale),
        out_shape=jax.ShapeDtypeStruct((copies, owned // 2, 2 * count), jnp.float32),
        compiler_params=SMALL_PARAMS,
    )(targets, slab)


def compress_body(owned, s_ref, a_ref, keep_ref, o_ref, inv_ref):
    groups = lax.axis_size(TGT)
    slabs = s_ref.shape[0] // groups
    count = groups * owned
    rows = []
    for t in range(groups):
        total = s_ref[t * slabs]
        for k in range(1, slabs):
            total = total + s_ref[t * slabs + k]
        rows += [total[:, :count], total[:, count:]]
    square = jnp.concatenate(rows, axis=0)
    square = 0.5 * (square + square.T)
    row = lax.broadcasted_iota(jnp.int32, (count, count), 0)
    col = lax.broadcasted_iota(jnp.int32, (count, count), 1)
    wide = jnp.concatenate([square, jnp.where(row == col, 1.0, 0.0)], axis=1)
    tiles = [wide[8 * t : 8 * t + 8] for t in range(count // 8)]
    sub = lax.broadcasted_iota(jnp.int32, (8, LANES), 0)
    down = lambda v, k: jnp.broadcast_to(v[k : k + 1], (8, LANES))
    for p in range(count // 8):
        later = range(p, count // 8)
        cols = {
            (t, k): jnp.broadcast_to(tiles[t][:, 8 * p + k : 8 * p + k + 1], (8, LANES))
            for t in later
            for k in range(8)
        }
        root = jnp.ones((8, LANES), jnp.float32)
        for k in range(8):
            pivot = down(cols[p, k], k)
            over = 1.0 / pivot
            root = jnp.where(sub == k, lax.rsqrt(pivot), root)
            line = down(tiles[p], k)
            cross = [down(cols[p, m], k) for m in range(k + 1, 8)]
            for t in later:
                f = cols[t, k] * over
                if t == p:
                    f = jnp.where(sub > k, f, 0.0)
                tiles[t] = tiles[t] - f * line
                for m in range(k + 1, 8):
                    cols[t, m] = cols[t, m] - f * cross[m - k - 1]
        inv_ref[8 * p : 8 * p + 8, :] = tiles[p] * root
    first = lax.axis_index(TGT) * owned
    mine = inv_ref[pl.ds(pl.multiple_of(first, 8), owned), :][:, count:]
    kept = first + lax.broadcasted_iota(jnp.int32, (owned, count), 0) < keep_ref[:owned, :count]
    mine = jnp.where(kept, mine, 0.0)
    for q in (0, 1):
        o_ref[:, q, :] = jnp.dot(
            mine,
            plane_of(a_ref, q),
            precision=lax.Precision.HIGHEST,
            preferred_element_type=jnp.float32,
        )


def compress(summands, slab, keep, owned):
    count = slab.shape[0] * owned
    vmem = pl.BlockSpec(memory_space=pltpu.VMEM)
    return pl.pallas_call(
        functools.partial(compress_body, owned),
        out_shape=jax.ShapeDtypeStruct((owned, 2, slab.shape[2]), jnp.float32),
        in_specs=[vmem] * 3,
        out_specs=vmem,
        scratch_shapes=[pltpu.VMEM((count, LANES), jnp.float32)],
        compiler_params=SMALL_PARAMS,
    )(summands, slab, keep)


def shards(targets, partners, occupied, retained):
    owned, n, plane = targets.shape
    consts = [jnp.asarray(c) for c in tables(n)]
    groups = lax.axis_size(TGT)
    swap = [(0, 1), (1, 0)]
    own_partners, keep = folded_partners(partners, occupied, retained)
    other_partners = lax.ppermute(own_partners, "core", swap)
    partial_actions, folded = solve(targets, own_partners, consts)
    cut = solve(folded, other_partners, consts, partial_actions)
    copies = spread(lax.all_to_all(cut, PTR, 0, 0, tiled=True), groups)
    slab = lax.all_to_all(copies, TGT, 0, 0, tiled=True)
    summands = overlap(targets, slab, lax.axis_size(TGT + PTR), 1.0 / n**3)
    summands = lax.all_to_all(summands, TGT + PTR, 0, 0, tiled=True)
    return compress(summands, slab, keep, owned)


def solution(mesh):
    names = TGT + PTR
    finer = Mesh(mesh.devices.reshape(2, 4, 4, 2, 2), names)
    in_specs = (P(TGT, None, None), P(None, None, PTR), P(PTR), P())
    out_specs = P(TGT, PTR, None)
    return jax.shard_map(
        shards, mesh=finer, in_specs=in_specs, out_specs=out_specs, check_vma=False
    )
```

```python
import functools

import jax
import jax.numpy as jnp
import ml_dtypes
import numpy as np
from jax import lax
from jax.experimental import pallas as pl
from jax.experimental.pallas import tpu as pltpu
from jax.sharding import Mesh
from jax.sharding import PartitionSpec as P

TGT = ("tgt_0", "tgt_1")
PTR = ("ptr_0", "ptr_1", "core")
LANES = 128
SOLVE_PARAMS = pltpu.CompilerParams(vmem_limit_bytes=24 << 20)
SMALL_PARAMS = pltpu.CompilerParams(vmem_limit_bytes=16 << 20)


def split_np(a):
    a = a.astype(np.float64)
    hi = a.astype(np.float32).astype(ml_dtypes.bfloat16)
    lo = (a - hi.astype(np.float64)).astype(np.float32).astype(ml_dtypes.bfloat16)
    return hi, lo


def half_bases(n):
    h = n // 2
    y = np.arange(h) + 0.5
    even_k, odd_k = np.arange(h), np.arange(1, h + 1)
    even = np.cos(2 * np.pi * even_k[:, None] * y[None] / n) * np.sqrt(2.0 / h)
    even[0] *= np.sqrt(0.5)
    odd = np.sin(2 * np.pi * odd_k[:, None] * y[None] / n) * np.sqrt(2.0 / h)
    odd[-1] *= np.sqrt(0.5)
    return (even, odd), (even_k, odd_k)


def tables(n):
    bases, freqs = half_bases(n)
    half = n // 2
    planes, kernels = [], []
    wave = lambda k: (k * (2 * np.pi / n)) ** 2
    ix = np.arange(half)
    weight = np.where(ix == 0, 1.0, 2.0) / half / 8
    for sy in (0, 1):
        for sz in (0, 1):
            m = np.einsum("ky,lz->yzkl", bases[sy], bases[sz])
            planes.append(m.reshape(half * half, half * half))
            for wx in (wave(ix), wave(half - ix)):
                total = wx[:, None, None] + wave(freqs[sy])[:, None] + wave(freqs[sz])[None]
                g = np.where(total > 0, 4 * np.pi / np.where(total > 0, total, 1.0), 0.0)
                kernels.append((g * weight[:, None, None]).reshape(half, -1, LANES))
    kernels = np.stack(kernels).reshape(4, n, -1, LANES).transpose(0, 2, 1, 3)
    return np.concatenate(split_np(np.stack(planes))), kernels.reshape(-1, n, LANES).astype(np.float32)


def split(v):
    hi = v.astype(jnp.bfloat16)
    return hi, (v - hi.astype(jnp.float32)).astype(jnp.bfloat16)


def dot(a, b):
    return jnp.dot(a, b, preferred_element_type=jnp.float32)


def dot_t(a, b):
    return lax.dot_general(a, b, (((1,), (1,)), ((), ())), preferred_element_type=jnp.float32)


def take(v, idx):
    return jnp.take_along_axis(v, idx, axis=1)


def fold(tiles, rows):
    lane = lax.broadcasted_iota(jnp.int32, (rows, LANES), 1)
    y, z = (lane // 16) % 4, lane % 16
    out = {}
    for sy in (0, 1):
        for sz in (0, 1):
            idx = (3 - y if sy else y) * 32 + (31 - z if sz else z)
            for h in (0, 1):
                a, b = (7 - 2 * h, 6 - 2 * h) if sy else (2 * h, 2 * h + 1)
                out[2 * sy + sz, h] = jnp.where(lane < 64, take(tiles[a], idx), take(tiles[b], idx))
    return out


def unfold(folded, rows):
    lane = lax.broadcasted_iota(jnp.int32, (rows, LANES), 1)
    y, z = lane // 32, lane % 32
    low = z < 16
    z = jnp.where(low, z, 31 - z)
    out = []
    for t in range(8):
        sy = t // 4
        h = (7 - t) // 2 if sy else t // 2
        first = 7 - 4 * (t % 2) if sy else 4 * (t % 2)
        idx = (first - y if sy else first + y) * 16 + z
        out.append(jnp.where(low, take(folded[2 * sy, h], idx), take(folded[2 * sy + 1, h], idx)))
    return out


def cosines(v):
    n = len(v)
    if n == 1:
        return v
    half = n // 2
    even = cosines([v[i] + v[n - 1 - i] for i in range(half)])
    if n == 2:
        return [even[0], (v[0] - v[1]) * np.float32(np.sqrt(0.5))]
    scale = [np.float32(2 * np.cos(np.pi * (2 * i + 1) / (2 * n))) for i in range(half)]
    odd = cosines([(v[i] - v[n - 1 - i]) * scale[i] for i in range(half)])
    out = [even[0], odd[0] * np.float32(0.5)]
    for k in range(1, half):
        out += [even[k], odd[k] - out[-1]]
    return out


def cosines_t(x):
    n = len(x)
    if n == 1:
        return x
    half = n // 2
    even = cosines_t(x[0::2])
    if n == 2:
        b = [x[1] * np.float32(np.sqrt(0.5))]
    else:
        z = [x[n - 1]]
        for k in range(half - 2, -1, -1):
            z.insert(0, x[2 * k + 1] - z[0])
        z[0] = z[0] * np.float32(0.5)
        scale = [np.float32(2 * np.cos(np.pi * (2 * i + 1) / (2 * n))) for i in range(half)]
        b = [c * w for c, w in zip(cosines_t(z), scale)]
    return [even[i] + b[i] for i in range(half)] + [even[i] - b[i] for i in range(half - 1, -1, -1)]


def along_x(v, table):
    half = len(v) // 2
    even = [v[i] + v[-1 - i] for i in range(half)]
    odd = [v[-1 - i] - v[i] if i % 2 else v[i] - v[-1 - i] for i in range(half)]
    even = cosines_t([c * table(k) for k, c in enumerate(cosines(even))])
    odd = cosines_t([c * table(half + k) for k, c in enumerate(cosines(odd))])
    low = [e - o if i % 2 else e + o for i, (e, o) in enumerate(zip(even, odd))]
    high = [e + o if i % 2 else e - o for i, (e, o) in enumerate(zip(even, odd))]
    return low + high[::-1]


def butterfly(d):
    a, b, c, e = d[0] + d[1], d[0] - d[1], d[2] + d[3], d[2] - d[3]
    return a + c, b + e, a - c, b - e


def fold_body(nj, n, p_ref, occ_ref, rank_ref, o_ref, keep_ref):
    keep_ref[...] = jnp.full(keep_ref.shape, rank_ref[0], jnp.int32)
    occ = jnp.full((n, LANES), occ_ref[0], jnp.int32).astype(jnp.float32)
    root = jnp.sqrt(0.25 + 0.75 * occ)
    lane = lax.broadcasted_iota(jnp.int32, (n, LANES), 1)
    part = lane // n
    tiles = [[] for _ in range(nj)]
    for t in range(n // nj):
        src = [p_ref[pl.ds(nj * t + y, n, stride=n), :] * root for y in range(nj)]
        for j in range(nj):
            acc = src[j]
            for y in range(nj):
                if y != j:
                    acc = jnp.where(part == y, pltpu.roll(src[y], ((y - j) % nj) * n, 1), acc)
            tiles[j].append(acc)
    for j in range(nj):
        for (s, h), v in fold(tiles[j], n).items():
            o_ref[2 * s + h, j * n : (j + 1) * n, :] = v


def folded_partners(partners, occupied, retained):
    n = partners.shape[0]
    nj = partners.shape[2] // n
    vmem = pl.BlockSpec(memory_space=pltpu.VMEM)
    smem = pl.BlockSpec(memory_space=pltpu.SMEM)
    return pl.pallas_call(
        functools.partial(fold_body, nj, n),
        out_shape=(
            jax.ShapeDtypeStruct((n * n // LANES, nj * n, LANES), jnp.float32),
            jax.ShapeDtypeStruct((8, LANES), jnp.int32),
        ),
        in_specs=[vmem, smem, smem],
        out_specs=(vmem, vmem),
        compiler_params=SMALL_PARAMS,
        cost_estimate=pl.CostEstimate(flops=2 << 30, bytes_accessed=8 << 20, transcendentals=0),
    )(partners.reshape(n * n, -1), occupied, retained)


def solve_body(last, tb, n, *refs):
    if last:
        t8, prior, p_ref, w_ref, k_ref, o_ref, p8, gh, gl, ps = refs
    else:
        t_ref, p_ref, w_ref, k_ref, o_ref, t8, p8, gh, gl, ps, rows_ref = refs
    quarter = n * n // 4
    tiles = n * n // LANES
    pairs = p8.shape[0]
    sub = lax.broadcasted_iota(jnp.int32, (8, LANES), 0)
    upper, second, late = sub < tb, sub % 2 == 1, sub % tb >= 2
    at = lambda k: slice(LANES * k, LANES * (k + 1))
    cls = lambda s: slice(quarter * s, quarter * (s + 1))
    if not last:
        first = lax.axis_index("core") * tb
        for i in range(tb):
            folded = fold([t_ref[first + i, :, at(k)] for k in range(tiles)], n)
            for (s, h), v in folded.items():
                rows_ref[2 * s + h, i * n : (i + 1) * n, :] = v
        for k in range(tiles):
            for x in range(n):
                rows = [rows_ref[k, pl.ds(i * n + x, 8, stride=0), :] for i in range(tb)]
                low, high = jnp.where(second, rows[1], rows[0]), jnp.where(second, rows[3], rows[2])
                t8[x, :, at(k)] = jnp.where(late, high, low)
    for g in range(pairs):
        for k in range(tiles):
            for x in range(n):
                a, b = (
                    p_ref[k, pl.ds(j * n + x, 8, stride=0), :] for j in (2 * g, 2 * g + 1)
                )
                p8[g, x, :, at(k)] = jnp.where(upper, a, b)
    for g in range(pairs):
        for x in range(0, n, 2):
            both = []
            for y in (x, x + 1):
                both.append(butterfly([t8[y, :, cls(s)] * p8[g, y, :, cls(s)] for s in range(4)]))
            q = slice((g * n + x) * 8, (g * n + x + 2) * 8)
            for s in range(4):
                gh[s, q, :], gl[s, q, :] = split(jnp.concatenate([both[0][s], both[1][s]], axis=0))

    def forward(s):
        ps[s] = dot(gh[s], w_ref[s]) + dot(gl[s], w_ref[s]) + dot(gh[s], w_ref[4 + s])

    def middle(s):
        for g in range(pairs):
            for h in range(quarter // LANES):
                v = [ps[s, (g * n + x) * 8 : (g * n + x + 1) * 8, at(h)] for x in range(n)]
                k = s * (quarter // LANES) + h
                v = along_x(v, lambda r, k=k: k_ref[k, pl.ds(r, 8, stride=0), :])
                for x in range(0, n, 2):
                    q = slice((g * n + x) * 8, (g * n + x + 2) * 8)
                    gh[s, q, at(h)], gl[s, q, at(h)] = split(jnp.concatenate(v[x : x + 2], axis=0))

    def back(s):
        ps[s] = dot_t(gh[s], w_ref[s]) + dot_t(gl[s], w_ref[s]) + dot_t(gh[s], w_ref[4 + s])

    forward(0)
    forward(1)
    middle(0)
    forward(2)
    middle(1)
    back(0)
    forward(3)
    middle(2)
    back(1)
    middle(3)
    back(2)
    back(3)
    done = []
    for x in range(n):
        acc = [prior[x, :, cls(s)] if last else None for s in range(4)]
        for g in range(pairs):
            q = slice((g * n + x) * 8, (g * n + x + 1) * 8)
            for s, v in enumerate(butterfly([ps[s, q, :] for s in range(4)])):
                v = v * p8[g, x, :, cls(s)]
                acc[s] = v if acc[s] is None else acc[s] + v
        if not last:
            for s in range(4):
                o_ref[x, :, cls(s)] = acc[s]
            continue
        done.append(acc)
        if len(done) == 2:
            folded = {}
            for s in range(4):
                for h in range(quarter // LANES):
                    a, b = (v[s][:, at(h)] for v in done)
                    folded[s, h] = jnp.where(upper, a, pltpu.roll(b, tb, 0)) + jnp.where(upper, pltpu.roll(a, tb, 0), b)
            for (c, h), v in folded.items():
                o_ref[x // 2, :, slice(quarter * c + LANES * h, quarter * c + LANES * (h + 1))] = v
            done = []


def solve(targets, partners, consts, prior=None):
    last = prior is not None
    tiles, rows, _ = partners.shape
    n, tb = 32, 4
    pairs = rows // n // 2
    vmem = pl.BlockSpec(memory_space=pltpu.VMEM)
    part = jax.ShapeDtypeStruct((n, 2 * tb, n * n), jnp.float32)
    if last:
        operands = (targets, prior, partners, *consts)
        out_shape = jax.ShapeDtypeStruct((n // 2, 2 * tb, n * n), jnp.float32)
    else:
        operands = (targets, partners, *consts)
        out_shape = (part, part)
    long = pairs * n * 2 * tb
    scratch = [
        pltpu.VMEM((pairs, n, 2 * tb, n * n), jnp.float32),
        pltpu.VMEM((4, long, n * n // 4), jnp.bfloat16),
        pltpu.VMEM((4, long, n * n // 4), jnp.bfloat16),
        pltpu.VMEM((4, long, n * n // 4), jnp.float32),
    ]
    if not last:
        scratch.append(pltpu.VMEM((tiles, tb * n, LANES), jnp.float32))
    return pl.pallas_call(
        functools.partial(solve_body, last, tb, n),
        out_shape=out_shape,
        in_specs=[vmem] * len(operands),
        out_specs=vmem if last else (vmem, vmem),
        scratch_shapes=scratch,
        compiler_params=SOLVE_PARAMS,
        cost_estimate=pl.CostEstimate(
            flops=2 * 6 * long * (n * n // 2) ** 2, bytes_accessed=8 << 20, transcendentals=0
        ),
    )(*operands)


def spread_body(in_ref, o_ref):
    peers, rows, _ = in_ref.shape
    halves = []
    for core in (0, 1):
        total = in_ref[core]
        for k in range(core + 2, peers, 2):
            total = total + in_ref[k]
        halves.append(total)
    order = [v[q * rows // 2 : (q + 1) * rows // 2] for q in (0, 1) for v in halves]
    slab = jnp.concatenate(order, axis=0)
    folded = {(k // 2, k % 2): slab[:, LANES * k : LANES * (k + 1)] for k in range(8)}
    slab = jnp.concatenate(unfold(folded, slab.shape[0]), axis=1)
    for k in range(o_ref.shape[0]):
        o_ref[k] = slab


def spread(received, copies):
    _, rows, plane = received.shape
    return pl.pallas_call(
        spread_body,
        out_shape=jax.ShapeDtypeStruct((copies, 2 * rows, plane), jnp.float32),
        compiler_params=SMALL_PARAMS,
    )(received)


def plane_of(ref, q):
    half = ref.shape[1] // 2
    return ref[:, q * half : (q + 1) * half, :].reshape(ref.shape[0] * half, ref.shape[2])


def overlap_body(scale, t_ref, a_ref, o_ref):
    owned = t_ref.shape[0]
    first = 2 * lax.axis_index(PTR)
    total = None
    for q in (0, 1):
        t = [t_ref[i, pl.ds(first + q, 1), :] for i in range(owned)]
        s = lax.dot_general(
            jnp.concatenate(t, axis=0),
            plane_of(a_ref, q),
            (((1,), (1,)), ((), ())),
            precision=lax.Precision.HIGHEST,
            preferred_element_type=jnp.float32,
        )
        total = s if total is None else total + s
    total = total * scale
    packed = jnp.concatenate([total[: owned // 2], total[owned // 2 :]], axis=1)
    for k in range(o_ref.shape[0]):
        o_ref[k] = packed


def overlap(targets, slab, copies, scale):
    owned = targets.shape[0]
    count = slab.shape[0] * owned
    return pl.pallas_call(
        functools.partial(overlap_body, scale),
        out_shape=jax.ShapeDtypeStruct((copies, owned // 2, 2 * count), jnp.float32),
        compiler_params=SMALL_PARAMS,
    )(targets, slab)


def compress_body(owned, s_ref, a_ref, keep_ref, o_ref, inv_ref):
    groups = lax.axis_size(TGT)
    slabs = s_ref.shape[0] // groups
    count = groups * owned
    rows = []
    for t in range(groups):
        total = s_ref[t * slabs]
        for k in range(1, slabs):
            total = total + s_ref[t * slabs + k]
        rows += [total[:, :count], total[:, count:]]
    square = jnp.concatenate(rows, axis=0)
    square = 0.5 * (square + square.T)
    row = lax.broadcasted_iota(jnp.int32, (count, count), 0)
    col = lax.broadcasted_iota(jnp.int32, (count, count), 1)
    wide = jnp.concatenate([square, jnp.where(row == col, 1.0, 0.0)], axis=1)
    tiles = [wide[8 * t : 8 * t + 8] for t in range(count // 8)]
    sub = lax.broadcasted_iota(jnp.int32, (8, LANES), 0)
    down = lambda v, k: jnp.broadcast_to(v[k : k + 1], (8, LANES))
    for p in range(count // 8):
        later = range(p, count // 8)
        cols = {
            (t, k): jnp.broadcast_to(tiles[t][:, 8 * p + k : 8 * p + k + 1], (8, LANES))
            for t in later
            for k in range(8)
        }
        root = jnp.ones((8, LANES), jnp.float32)
        for k in range(0, 8, 2):
            first, second = cols[p, k], cols[p, k + 1]
            a, b, d = down(first, k), down(second, k), down(second, k + 1)
            over = 1.0 / a
            pivot = d - b * (b * over)
            under = a * (1.0 / (a * d - b * b))
            ratio = b * over
            root = jnp.where(sub == k, lax.rsqrt(a), jnp.where(sub == k + 1, lax.rsqrt(pivot), root))
            line, next_line = down(tiles[p], k), down(tiles[p], k + 1)
            next_line = next_line - ratio * line
            cross = [(down(cols[p, m], k), down(cols[p, m], k + 1)) for m in range(k + 2, 8)]
            cross = [(u, v - ratio * u) for u, v in cross]
            for t in later:
                f = cols[t, k] * over
                g = (cols[t, k + 1] - cols[t, k] * ratio) * under
                if t == p:
                    f = jnp.where(sub > k, f, 0.0)
                    g = jnp.where(sub > k + 1, g, 0.0)
                tiles[t] = tiles[t] - f * line - g * next_line
                for m in range(k + 2, 8):
                    u, v = cross[m - k - 2]
                    cols[t, m] = cols[t, m] - f * u - g * v
        inv_ref[8 * p : 8 * p + 8, :] = tiles[p] * root
    first = lax.axis_index(TGT) * owned
    mine = inv_ref[pl.ds(pl.multiple_of(first, 8), owned), :][:, count:]
    kept = first + lax.broadcasted_iota(jnp.int32, (owned, count), 0) < keep_ref[:owned, :count]
    mine = jnp.where(kept, mine, 0.0)
    for q in (0, 1):
        o_ref[:, q, :] = jnp.dot(
            mine,
            plane_of(a_ref, q),
            precision=lax.Precision.HIGHEST,
            preferred_element_type=jnp.float32,
        )


def compress(summands, slab, keep, owned):
    count = slab.shape[0] * owned
    vmem = pl.BlockSpec(memory_space=pltpu.VMEM)
    return pl.pallas_call(
        functools.partial(compress_body, owned),
        out_shape=jax.ShapeDtypeStruct((owned, 2, slab.shape[2]), jnp.float32),
        in_specs=[vmem] * 3,
        out_specs=vmem,
        scratch_shapes=[pltpu.VMEM((count, LANES), jnp.float32)],
        compiler_params=SMALL_PARAMS,
    )(summands, slab, keep)


def shards(targets, partners, occupied, retained):
    owned, n, plane = targets.shape
    consts = [jnp.asarray(c) for c in tables(n)]
    groups = lax.axis_size(TGT)
    swap = [(0, 1), (1, 0)]
    own_partners, keep = folded_partners(partners, occupied, retained)
    other_partners = lax.ppermute(own_partners, "core", swap)
    partial_actions, folded = solve(targets, own_partners, consts)
    cut = solve(folded, other_partners, consts, partial_actions)
    copies = spread(lax.all_to_all(cut, PTR, 0, 0, tiled=True), groups)
    slab = lax.all_to_all(copies, TGT, 0, 0, tiled=True)
    summands = overlap(targets, slab, lax.axis_size(TGT + PTR), 1.0 / n**3)
    summands = lax.all_to_all(summands, TGT + PTR, 0, 0, tiled=True)
    return compress(summands, slab, keep, owned)


def solution(mesh):
    names = TGT + PTR
    finer = Mesh(mesh.devices.reshape(2, 4, 4, 2, 2), names)
    in_specs = (P(TGT, None, None), P(None, None, PTR), P(PTR), P())
    out_specs = P(TGT, PTR, None)
    return jax.shard_map(
        shards, mesh=finer, in_specs=in_specs, out_specs=out_specs, check_vma=False
    )
```

```python
import functools

import jax
import jax.numpy as jnp
import ml_dtypes
import numpy as np
from jax import lax
from jax.experimental import pallas as pl
from jax.experimental.pallas import tpu as pltpu
from jax.sharding import Mesh
from jax.sharding import PartitionSpec as P

TGT = ("tgt_0", "tgt_1")
PTR = ("ptr_0", "ptr_1", "core")
LANES = 128
SOLVE_PARAMS = pltpu.CompilerParams(vmem_limit_bytes=24 << 20)
SMALL_PARAMS = pltpu.CompilerParams(vmem_limit_bytes=16 << 20)


def split_np(a):
    a = a.astype(np.float64)
    hi = a.astype(np.float32).astype(ml_dtypes.bfloat16)
    lo = (a - hi.astype(np.float64)).astype(np.float32).astype(ml_dtypes.bfloat16)
    return hi, lo


def half_bases(n):
    h = n // 2
    y = np.arange(h) + 0.5
    even_k, odd_k = np.arange(h), np.arange(1, h + 1)
    even = np.cos(2 * np.pi * even_k[:, None] * y[None] / n) * np.sqrt(2.0 / h)
    even[0] *= np.sqrt(0.5)
    odd = np.sin(2 * np.pi * odd_k[:, None] * y[None] / n) * np.sqrt(2.0 / h)
    odd[-1] *= np.sqrt(0.5)
    return (even, odd), (even_k, odd_k)


def tables(n):
    bases, freqs = half_bases(n)
    half = n // 2
    planes, kernels = [], []
    wave = lambda k: (k * (2 * np.pi / n)) ** 2
    ix = np.arange(half)
    weight = np.where(ix == 0, 1.0, 2.0) / half / 8
    for sy in (0, 1):
        for sz in (0, 1):
            m = np.einsum("ky,lz->yzkl", bases[sy], bases[sz])
            planes.append(m.reshape(half * half, half * half))
            for wx in (wave(ix), wave(half - ix)):
                total = wx[:, None, None] + wave(freqs[sy])[:, None] + wave(freqs[sz])[None]
                g = np.where(total > 0, 4 * np.pi / np.where(total > 0, total, 1.0), 0.0)
                kernels.append((g * weight[:, None, None]).reshape(half, -1, LANES))
    kernels = np.stack(kernels).reshape(4, n, -1, LANES).transpose(0, 2, 1, 3)
    return np.concatenate(split_np(np.stack(planes))), kernels.reshape(-1, n, LANES).astype(np.float32)


def split(v):
    hi = v.astype(jnp.bfloat16)
    return hi, (v - hi.astype(jnp.float32)).astype(jnp.bfloat16)


def dot(a, b):
    return jnp.dot(a, b, preferred_element_type=jnp.float32)


def dot_t(a, b):
    return lax.dot_general(a, b, (((1,), (1,)), ((), ())), preferred_element_type=jnp.float32)


def take(v, idx):
    return jnp.take_along_axis(v, idx, axis=1)


def fold(tiles, rows):
    lane = lax.broadcasted_iota(jnp.int32, (rows, LANES), 1)
    y, z = (lane // 16) % 4, lane % 16
    out = {}
    for sy in (0, 1):
        for sz in (0, 1):
            idx = (3 - y if sy else y) * 32 + (31 - z if sz else z)
            for h in (0, 1):
                a, b = (7 - 2 * h, 6 - 2 * h) if sy else (2 * h, 2 * h + 1)
                out[2 * sy + sz, h] = jnp.where(lane < 64, take(tiles[a], idx), take(tiles[b], idx))
    return out


def unfold(folded, rows):
    lane = lax.broadcasted_iota(jnp.int32, (rows, LANES), 1)
    y, z = lane // 32, lane % 32
    low = z < 16
    z = jnp.where(low, z, 31 - z)
    out = []
    for t in range(8):
        sy = t // 4
        h = (7 - t) // 2 if sy else t // 2
        first = 7 - 4 * (t % 2) if sy else 4 * (t % 2)
        idx = (first - y if sy else first + y) * 16 + z
        out.append(jnp.where(low, take(folded[2 * sy, h], idx), take(folded[2 * sy + 1, h], idx)))
    return out


def cosines(v):
    n = len(v)
    if n == 1:
        return v
    half = n // 2
    even = cosines([v[i] + v[n - 1 - i] for i in range(half)])
    if n == 2:
        return [even[0], (v[0] - v[1]) * np.float32(np.sqrt(0.5))]
    scale = [np.float32(2 * np.cos(np.pi * (2 * i + 1) / (2 * n))) for i in range(half)]
    odd = cosines([(v[i] - v[n - 1 - i]) * scale[i] for i in range(half)])
    out = [even[0], odd[0] * np.float32(0.5)]
    for k in range(1, half):
        out += [even[k], odd[k] - out[-1]]
    return out


def cosines_t(x):
    n = len(x)
    if n == 1:
        return x
    half = n // 2
    even = cosines_t(x[0::2])
    if n == 2:
        b = [x[1] * np.float32(np.sqrt(0.5))]
    else:
        z = [x[n - 1]]
        for k in range(half - 2, -1, -1):
            z.insert(0, x[2 * k + 1] - z[0])
        z[0] = z[0] * np.float32(0.5)
        scale = [np.float32(2 * np.cos(np.pi * (2 * i + 1) / (2 * n))) for i in range(half)]
        b = [c * w for c, w in zip(cosines_t(z), scale)]
    return [even[i] + b[i] for i in range(half)] + [even[i] - b[i] for i in range(half - 1, -1, -1)]


def along_x(v, table):
    half = len(v) // 2
    even = [v[i] + v[-1 - i] for i in range(half)]
    odd = [v[-1 - i] - v[i] if i % 2 else v[i] - v[-1 - i] for i in range(half)]
    even = cosines_t([c * table(k) for k, c in enumerate(cosines(even))])
    odd = cosines_t([c * table(half + k) for k, c in enumerate(cosines(odd))])
    low = [e - o if i % 2 else e + o for i, (e, o) in enumerate(zip(even, odd))]
    high = [e + o if i % 2 else e - o for i, (e, o) in enumerate(zip(even, odd))]
    return low + high[::-1]


def butterfly(d):
    a, b, c, e = d[0] + d[1], d[0] - d[1], d[2] + d[3], d[2] - d[3]
    return a + c, b + e, a - c, b - e


def fold_body(nj, n, p_ref, occ_ref, rank_ref, o_ref, keep_ref):
    keep_ref[...] = jnp.full(keep_ref.shape, rank_ref[0], jnp.int32)
    occ = jnp.full((n, LANES), occ_ref[0], jnp.int32).astype(jnp.float32)
    root = jnp.sqrt(0.25 + 0.75 * occ)
    lane = lax.broadcasted_iota(jnp.int32, (n, LANES), 1)
    part = lane // n
    tiles = [[] for _ in range(nj)]
    for t in range(n // nj):
        src = [p_ref[pl.ds(nj * t + y, n, stride=n), :] * root for y in range(nj)]
        for j in range(nj):
            acc = src[j]
            for y in range(nj):
                if y != j:
                    acc = jnp.where(part == y, pltpu.roll(src[y], ((y - j) % nj) * n, 1), acc)
            tiles[j].append(acc)
    for j in range(nj):
        for (s, h), v in fold(tiles[j], n).items():
            o_ref[2 * s + h, j * n : (j + 1) * n, :] = v


def folded_partners(partners, occupied, retained):
    n = partners.shape[0]
    nj = partners.shape[2] // n
    vmem = pl.BlockSpec(memory_space=pltpu.VMEM)
    smem = pl.BlockSpec(memory_space=pltpu.SMEM)
    return pl.pallas_call(
        functools.partial(fold_body, nj, n),
        out_shape=(
            jax.ShapeDtypeStruct((n * n // LANES, nj * n, LANES), jnp.float32),
            jax.ShapeDtypeStruct((8, LANES), jnp.int32),
        ),
        in_specs=[vmem, smem, smem],
        out_specs=(vmem, vmem),
        compiler_params=SMALL_PARAMS,
        cost_estimate=pl.CostEstimate(flops=2 << 30, bytes_accessed=8 << 20, transcendentals=0),
    )(partners.reshape(n * n, -1), occupied, retained)


def solve_body(last, tb, n, *refs):
    if last:
        t8, prior, p_ref, w_ref, k_ref, o_ref, p8, gh, gl, ps = refs
    else:
        t_ref, p_ref, w_ref, k_ref, o_ref, t8, p8, gh, gl, ps, rows_ref = refs
    quarter = n * n // 4
    tiles = n * n // LANES
    pairs = p8.shape[0]
    sub = lax.broadcasted_iota(jnp.int32, (8, LANES), 0)
    upper, second, late = sub < tb, sub % 2 == 1, sub % tb >= 2
    at = lambda k: slice(LANES * k, LANES * (k + 1))
    cls = lambda s: slice(quarter * s, quarter * (s + 1))
    if not last:
        first = lax.axis_index("core") * tb
        for i in range(tb):
            folded = fold([t_ref[first + i, :, at(k)] for k in range(tiles)], n)
            for (s, h), v in folded.items():
                rows_ref[2 * s + h, i * n : (i + 1) * n, :] = v
        for k in range(tiles):
            for x in range(n):
                rows = [rows_ref[k, pl.ds(i * n + x, 8, stride=0), :] for i in range(tb)]
                low, high = jnp.where(second, rows[1], rows[0]), jnp.where(second, rows[3], rows[2])
                t8[x, :, at(k)] = jnp.where(late, high, low)
    for g in range(pairs):
        for k in range(tiles):
            for x in range(n):
                a, b = (
                    p_ref[k, pl.ds(j * n + x, 8, stride=0), :] for j in (2 * g, 2 * g + 1)
                )
                p8[g, x, :, at(k)] = jnp.where(upper, a, b)
    for g in range(pairs):
        for x in range(0, n, 2):
            both = []
            for y in (x, x + 1):
                both.append(butterfly([t8[y, :, cls(s)] * p8[g, y, :, cls(s)] for s in range(4)]))
            q = slice((g * n + x) * 8, (g * n + x + 2) * 8)
            for s in range(4):
                gh[s, q, :], gl[s, q, :] = split(jnp.concatenate([both[0][s], both[1][s]], axis=0))

    def forward(s):
        ps[s] = dot(gh[s], w_ref[s]) + dot(gl[s], w_ref[s]) + dot(gh[s], w_ref[4 + s])

    def middle(s):
        for g in range(pairs):
            for h in range(quarter // LANES):
                v = [ps[s, (g * n + x) * 8 : (g * n + x + 1) * 8, at(h)] for x in range(n)]
                k = s * (quarter // LANES) + h
                v = along_x(v, lambda r, k=k: k_ref[k, pl.ds(r, 8, stride=0), :])
                for x in range(0, n, 2):
                    q = slice((g * n + x) * 8, (g * n + x + 2) * 8)
                    gh[s, q, at(h)], gl[s, q, at(h)] = split(jnp.concatenate(v[x : x + 2], axis=0))

    def back(s):
        ps[s] = dot_t(gh[s], w_ref[s]) + dot_t(gl[s], w_ref[s]) + dot_t(gh[s], w_ref[4 + s])

    steps = "ffffmmmmbbbb" if last else "ffmfmbfmbmbb"
    seen = dict.fromkeys("fmb", 0)
    for step in steps:
        {"f": forward, "m": middle, "b": back}[step](seen[step])
        seen[step] += 1
    done = []
    for x in range(n):
        acc = [prior[x, :, cls(s)] if last else None for s in range(4)]
        for g in range(pairs):
            q = slice((g * n + x) * 8, (g * n + x + 1) * 8)
            for s, v in enumerate(butterfly([ps[s, q, :] for s in range(4)])):
                v = v * p8[g, x, :, cls(s)]
                acc[s] = v if acc[s] is None else acc[s] + v
        if not last:
            for s in range(4):
                o_ref[x, :, cls(s)] = acc[s]
            continue
        done.append(acc)
        if len(done) == 2:
            folded = {}
            for s in range(4):
                for h in range(quarter // LANES):
                    a, b = (v[s][:, at(h)] for v in done)
                    folded[s, h] = jnp.where(upper, a, pltpu.roll(b, tb, 0)) + jnp.where(upper, pltpu.roll(a, tb, 0), b)
            for (c, h), v in folded.items():
                o_ref[x // 2, :, slice(quarter * c + LANES * h, quarter * c + LANES * (h + 1))] = v
            done = []


def solve(targets, partners, consts, prior=None):
    last = prior is not None
    tiles, rows, _ = partners.shape
    n, tb = 32, 4
    pairs = rows // n // 2
    vmem = pl.BlockSpec(memory_space=pltpu.VMEM)
    part = jax.ShapeDtypeStruct((n, 2 * tb, n * n), jnp.float32)
    if last:
        operands = (targets, prior, partners, *consts)
        out_shape = jax.ShapeDtypeStruct((n // 2, 2 * tb, n * n), jnp.float32)
    else:
        operands = (targets, partners, *consts)
        out_shape = (part, part)
    long = pairs * n * 2 * tb
    scratch = [
        pltpu.VMEM((pairs, n, 2 * tb, n * n), jnp.float32),
        pltpu.VMEM((4, long, n * n // 4), jnp.bfloat16),
        pltpu.VMEM((4, long, n * n // 4), jnp.bfloat16),
        pltpu.VMEM((4, long, n * n // 4), jnp.float32),
    ]
    if not last:
        scratch.append(pltpu.VMEM((tiles, tb * n, LANES), jnp.float32))
    return pl.pallas_call(
        functools.partial(solve_body, last, tb, n),
        out_shape=out_shape,
        in_specs=[vmem] * len(operands),
        out_specs=vmem if last else (vmem, vmem),
        scratch_shapes=scratch,
        compiler_params=SOLVE_PARAMS,
        cost_estimate=pl.CostEstimate(
            flops=2 * 6 * long * (n * n // 2) ** 2, bytes_accessed=8 << 20, transcendentals=0
        ),
    )(*operands)


def spread_body(in_ref, o_ref):
    peers, rows, _ = in_ref.shape
    halves = []
    for core in (0, 1):
        total = in_ref[core]
        for k in range(core + 2, peers, 2):
            total = total + in_ref[k]
        halves.append(total)
    order = [v[q * rows // 2 : (q + 1) * rows // 2] for q in (0, 1) for v in halves]
    slab = jnp.concatenate(order, axis=0)
    folded = {(k // 2, k % 2): slab[:, LANES * k : LANES * (k + 1)] for k in range(8)}
    slab = jnp.concatenate(unfold(folded, slab.shape[0]), axis=1)
    for k in range(o_ref.shape[0]):
        o_ref[k] = slab


def spread(received, copies):
    _, rows, plane = received.shape
    return pl.pallas_call(
        spread_body,
        out_shape=jax.ShapeDtypeStruct((copies, 2 * rows, plane), jnp.float32),
        compiler_params=SMALL_PARAMS,
    )(received)


def plane_of(ref, q):
    half = ref.shape[1] // 2
    return ref[:, q * half : (q + 1) * half, :].reshape(ref.shape[0] * half, ref.shape[2])


def overlap_body(scale, t_ref, a_ref, o_ref):
    owned = t_ref.shape[0]
    first = 2 * lax.axis_index(PTR)
    total = None
    for q in (0, 1):
        t = [t_ref[i, pl.ds(first + q, 1), :] for i in range(owned)]
        s = lax.dot_general(
            jnp.concatenate(t, axis=0),
            plane_of(a_ref, q),
            (((1,), (1,)), ((), ())),
            precision=lax.Precision.HIGHEST,
            preferred_element_type=jnp.float32,
        )
        total = s if total is None else total + s
    total = total * scale
    packed = jnp.concatenate([total[: owned // 2], total[owned // 2 :]], axis=1)
    for k in range(o_ref.shape[0]):
        o_ref[k] = packed


def overlap(targets, slab, copies, scale):
    owned = targets.shape[0]
    count = slab.shape[0] * owned
    return pl.pallas_call(
        functools.partial(overlap_body, scale),
        out_shape=jax.ShapeDtypeStruct((copies, owned // 2, 2 * count), jnp.float32),
        compiler_params=SMALL_PARAMS,
    )(targets, slab)


def compress_body(owned, s_ref, a_ref, keep_ref, o_ref, inv_ref):
    groups = lax.axis_size(TGT)
    slabs = s_ref.shape[0] // groups
    count = groups * owned
    rows = []
    for t in range(groups):
        total = s_ref[t * slabs]
        for k in range(1, slabs):
            total = total + s_ref[t * slabs + k]
        rows += [total[:, :count], total[:, count:]]
    square = jnp.concatenate(rows, axis=0)
    square = 0.5 * (square + square.T)
    row = lax.broadcasted_iota(jnp.int32, (count, count), 0)
    col = lax.broadcasted_iota(jnp.int32, (count, count), 1)
    wide = jnp.concatenate([square, jnp.where(row == col, 1.0, 0.0)], axis=1)
    tiles = [wide[8 * t : 8 * t + 8] for t in range(count // 8)]
    sub = lax.broadcasted_iota(jnp.int32, (8, LANES), 0)
    down = lambda v, k: jnp.broadcast_to(v[k : k + 1], (8, LANES))
    wide_panel = 16
    tops = count // 8
    roots = [jnp.ones((8, LANES), jnp.float32)] * tops
    for p in range(0, count, wide_panel):
        cols = {
            (t, k): jnp.broadcast_to(tiles[t][:, k : k + 1], (8, LANES))
            for t in range(p // 8, tops)
            for k in range(p, p + wide_panel)
        }
        for k in range(p, p + wide_panel, 2):
            top, r = k // 8, k % 8
            one, two = cols[top, k], cols[top, k + 1]
            a, b, d = down(one, r), down(two, r), down(two, r + 1)
            over = 1.0 / a
            under = a * (1.0 / (a * d - b * b))
            ratio = b * over
            pivot = d - b * ratio
            roots[top] = jnp.where(sub == r, lax.rsqrt(a), jnp.where(sub == r + 1, lax.rsqrt(pivot), roots[top]))
            line = down(tiles[top], r)
            next_line = down(tiles[top], r + 1) - ratio * line
            rest = range(k + 2, p + wide_panel)
            cross = {m: (down(cols[top, m], r), down(cols[top, m], r + 1)) for m in rest}
            cross = {m: (u, v - ratio * u) for m, (u, v) in cross.items()}
            for t in range(top, tops):
                f = cols[t, k] * over
                g = (cols[t, k + 1] - cols[t, k] * ratio) * under
                if t == top:
                    f = jnp.where(sub > r, f, 0.0)
                    g = jnp.where(sub > r + 1, g, 0.0)
                tiles[t] = tiles[t] - f * line - g * next_line
                for m in rest:
                    u, v = cross[m]
                    cols[t, m] = cols[t, m] - f * u - g * v
    for t in range(tops):
        inv_ref[8 * t : 8 * t + 8, :] = tiles[t] * roots[t]
    first = lax.axis_index(TGT) * owned
    mine = inv_ref[pl.ds(pl.multiple_of(first, 8), owned), :][:, count:]
    kept = first + lax.broadcasted_iota(jnp.int32, (owned, count), 0) < keep_ref[:owned, :count]
    mine = jnp.where(kept, mine, 0.0)
    for q in (0, 1):
        o_ref[:, q, :] = jnp.dot(
            mine,
            plane_of(a_ref, q),
            precision=lax.Precision.HIGHEST,
            preferred_element_type=jnp.float32,
        )


def compress(summands, slab, keep, owned):
    count = slab.shape[0] * owned
    vmem = pl.BlockSpec(memory_space=pltpu.VMEM)
    return pl.pallas_call(
        functools.partial(compress_body, owned),
        out_shape=jax.ShapeDtypeStruct((owned, 2, slab.shape[2]), jnp.float32),
        in_specs=[vmem] * 3,
        out_specs=vmem,
        scratch_shapes=[pltpu.VMEM((count, LANES), jnp.float32)],
        compiler_params=SMALL_PARAMS,
    )(summands, slab, keep)


def shards(targets, partners, occupied, retained):
    owned, n, plane = targets.shape
    consts = [jnp.asarray(c) for c in tables(n)]
    groups = lax.axis_size(TGT)
    swap = [(0, 1), (1, 0)]
    own_partners, keep = folded_partners(partners, occupied, retained)
    other_partners = lax.ppermute(own_partners, "core", swap)
    partial_actions, folded = solve(targets, own_partners, consts)
    cut = solve(folded, other_partners, consts, partial_actions)
    copies = spread(lax.all_to_all(cut, PTR, 0, 0, tiled=True), groups)
    slab = lax.all_to_all(copies, TGT, 0, 0, tiled=True)
    summands = overlap(targets, slab, lax.axis_size(TGT + PTR), 1.0 / n**3)
    summands = lax.all_to_all(summands, TGT + PTR, 0, 0, tiled=True)
    return compress(summands, slab, keep, owned)


def solution(mesh):
    names = TGT + PTR
    finer = Mesh(mesh.devices.reshape(2, 4, 4, 2, 2), names)
    in_specs = (P(TGT, None, None), P(None, None, PTR), P(PTR), P())
    out_specs = P(TGT, PTR, None)
    return jax.shard_map(
        shards, mesh=finer, in_specs=in_specs, out_specs=out_specs, check_vma=False
    )
```

```python
import functools

import jax
import jax.numpy as jnp
import ml_dtypes
import numpy as np
from jax import lax
from jax.experimental import pallas as pl
from jax.experimental.pallas import tpu as pltpu
from jax.sharding import Mesh
from jax.sharding import PartitionSpec as P

TGT = ("tgt_0", "tgt_1")
PTR = ("ptr_0", "ptr_1", "core")
LANES = 128
SOLVE_PARAMS = pltpu.CompilerParams(vmem_limit_bytes=24 << 20)
SMALL_PARAMS = pltpu.CompilerParams(vmem_limit_bytes=16 << 20)


def split_np(a):
    a = a.astype(np.float64)
    hi = a.astype(np.float32).astype(ml_dtypes.bfloat16)
    lo = (a - hi.astype(np.float64)).astype(np.float32).astype(ml_dtypes.bfloat16)
    return hi, lo


def half_bases(n):
    h = n // 2
    y = np.arange(h) + 0.5
    even_k, odd_k = np.arange(h), np.arange(1, h + 1)
    even = np.cos(2 * np.pi * even_k[:, None] * y[None] / n) * np.sqrt(2.0 / h)
    even[0] *= np.sqrt(0.5)
    odd = np.sin(2 * np.pi * odd_k[:, None] * y[None] / n) * np.sqrt(2.0 / h)
    odd[-1] *= np.sqrt(0.5)
    return (even, odd), (even_k, odd_k)


def tables(n):
    bases, freqs = half_bases(n)
    half = n // 2
    planes, kernels = [], []
    wave = lambda k: (k * (2 * np.pi / n)) ** 2
    ix = np.arange(half)
    weight = np.where(ix == 0, 1.0, 2.0) / half / 8
    for sy in (0, 1):
        for sz in (0, 1):
            m = np.einsum("ky,lz->yzkl", bases[sy], bases[sz])
            planes.append(m.reshape(half * half, half * half))
            for wx in (wave(ix), wave(half - ix)):
                total = wx[:, None, None] + wave(freqs[sy])[:, None] + wave(freqs[sz])[None]
                g = np.where(total > 0, 4 * np.pi / np.where(total > 0, total, 1.0), 0.0)
                kernels.append((g * weight[:, None, None]).reshape(half, -1, LANES))
    kernels = np.stack(kernels).reshape(4, n, -1, LANES).transpose(0, 2, 1, 3)
    return np.concatenate(split_np(np.stack(planes))), kernels.reshape(-1, n, LANES).astype(np.float32)


def split(v):
    hi = v.astype(jnp.bfloat16)
    return hi, (v - hi.astype(jnp.float32)).astype(jnp.bfloat16)


def dot(a, b):
    return jnp.dot(a, b, preferred_element_type=jnp.float32)


def dot_t(a, b):
    return lax.dot_general(a, b, (((1,), (1,)), ((), ())), preferred_element_type=jnp.float32)


def take(v, idx):
    return jnp.take_along_axis(v, idx, axis=1)


def fold(tiles, rows):
    lane = lax.broadcasted_iota(jnp.int32, (rows, LANES), 1)
    y, z = (lane // 16) % 4, lane % 16
    out = {}
    for sy in (0, 1):
        for sz in (0, 1):
            idx = (3 - y if sy else y) * 32 + (31 - z if sz else z)
            for h in (0, 1):
                a, b = (7 - 2 * h, 6 - 2 * h) if sy else (2 * h, 2 * h + 1)
                out[2 * sy + sz, h] = jnp.where(lane < 64, take(tiles[a], idx), take(tiles[b], idx))
    return out


def unfold(folded, rows):
    lane = lax.broadcasted_iota(jnp.int32, (rows, LANES), 1)
    y, z = lane // 32, lane % 32
    low = z < 16
    z = jnp.where(low, z, 31 - z)
    out = []
    for t in range(8):
        sy = t // 4
        h = (7 - t) // 2 if sy else t // 2
        first = 7 - 4 * (t % 2) if sy else 4 * (t % 2)
        idx = (first - y if sy else first + y) * 16 + z
        out.append(jnp.where(low, take(folded[2 * sy, h], idx), take(folded[2 * sy + 1, h], idx)))
    return out


def cosines(v):
    n = len(v)
    if n == 1:
        return v
    half = n // 2
    even = cosines([v[i] + v[n - 1 - i] for i in range(half)])
    if n == 2:
        return [even[0], (v[0] - v[1]) * np.float32(np.sqrt(0.5))]
    scale = [np.float32(2 * np.cos(np.pi * (2 * i + 1) / (2 * n))) for i in range(half)]
    odd = cosines([(v[i] - v[n - 1 - i]) * scale[i] for i in range(half)])
    out = [even[0], odd[0] * np.float32(0.5)]
    for k in range(1, half):
        out += [even[k], odd[k] - out[-1]]
    return out


def cosines_t(x):
    n = len(x)
    if n == 1:
        return x
    half = n // 2
    even = cosines_t(x[0::2])
    if n == 2:
        b = [x[1] * np.float32(np.sqrt(0.5))]
    else:
        z = [x[n - 1]]
        for k in range(half - 2, -1, -1):
            z.insert(0, x[2 * k + 1] - z[0])
        z[0] = z[0] * np.float32(0.5)
        scale = [np.float32(2 * np.cos(np.pi * (2 * i + 1) / (2 * n))) for i in range(half)]
        b = [c * w for c, w in zip(cosines_t(z), scale)]
    return [even[i] + b[i] for i in range(half)] + [even[i] - b[i] for i in range(half - 1, -1, -1)]


def along_x(v, table):
    half = len(v) // 2
    even = [v[i] + v[-1 - i] for i in range(half)]
    odd = [v[-1 - i] - v[i] if i % 2 else v[i] - v[-1 - i] for i in range(half)]
    even = cosines_t([c * table(k) for k, c in enumerate(cosines(even))])
    odd = cosines_t([c * table(half + k) for k, c in enumerate(cosines(odd))])
    low = [e - o if i % 2 else e + o for i, (e, o) in enumerate(zip(even, odd))]
    high = [e + o if i % 2 else e - o for i, (e, o) in enumerate(zip(even, odd))]
    return low + high[::-1]


def butterfly(d):
    a, b, c, e = d[0] + d[1], d[0] - d[1], d[2] + d[3], d[2] - d[3]
    return a + c, b + e, a - c, b - e


def fold_body(nj, n, p_ref, occ_ref, rank_ref, o_ref, keep_ref):
    keep_ref[...] = jnp.full(keep_ref.shape, rank_ref[0], jnp.int32)
    occ = jnp.full((n, LANES), occ_ref[0], jnp.int32).astype(jnp.float32)
    root = jnp.sqrt(0.25 + 0.75 * occ)
    lane = lax.broadcasted_iota(jnp.int32, (n, LANES), 1)
    part = lane // n
    tiles = [[] for _ in range(nj)]
    for t in range(n // nj):
        src = [p_ref[pl.ds(nj * t + y, n, stride=n), :] * root for y in range(nj)]
        for j in range(nj):
            acc = src[j]
            for y in range(nj):
                if y != j:
                    acc = jnp.where(part == y, pltpu.roll(src[y], ((y - j) % nj) * n, 1), acc)
            tiles[j].append(acc)
    for j in range(nj):
        for (s, h), v in fold(tiles[j], n).items():
            o_ref[2 * s + h, j * n : (j + 1) * n, :] = v


def folded_partners(partners, occupied, retained):
    n = partners.shape[0]
    nj = partners.shape[2] // n
    vmem = pl.BlockSpec(memory_space=pltpu.VMEM)
    smem = pl.BlockSpec(memory_space=pltpu.SMEM)
    return pl.pallas_call(
        functools.partial(fold_body, nj, n),
        out_shape=(
            jax.ShapeDtypeStruct((n * n // LANES, nj * n, LANES), jnp.float32),
            jax.ShapeDtypeStruct((8, LANES), jnp.int32),
        ),
        in_specs=[vmem, smem, smem],
        out_specs=(vmem, vmem),
        compiler_params=SMALL_PARAMS,
        cost_estimate=pl.CostEstimate(flops=2 << 30, bytes_accessed=8 << 20, transcendentals=0),
    )(partners.reshape(n * n, -1), occupied, retained)


def solve_body(last, tb, n, *refs):
    if last:
        t8, prior, p_ref, w_ref, k_ref, o_ref, p8, gh, gl, ps = refs
    else:
        t_ref, p_ref, w_ref, k_ref, o_ref, t8, p8, gh, gl, ps, rows_ref = refs
    quarter = n * n // 4
    tiles = n * n // LANES
    pairs = p8.shape[0]
    sub = lax.broadcasted_iota(jnp.int32, (8, LANES), 0)
    upper, second, late = sub < tb, sub % 2 == 1, sub % tb >= 2
    at = lambda k: slice(LANES * k, LANES * (k + 1))
    cls = lambda s: slice(quarter * s, quarter * (s + 1))
    if not last:
        first = lax.axis_index("core") * tb
        for i in range(tb):
            folded = fold([t_ref[first + i, :, at(k)] for k in range(tiles)], n)
            for (s, h), v in folded.items():
                rows_ref[2 * s + h, i * n : (i + 1) * n, :] = v
        for k in range(tiles):
            for x in range(n):
                rows = [rows_ref[k, pl.ds(i * n + x, 8, stride=0), :] for i in range(tb)]
                low, high = jnp.where(second, rows[1], rows[0]), jnp.where(second, rows[3], rows[2])
                t8[x, :, at(k)] = jnp.where(late, high, low)
    for g in range(pairs):
        for k in range(tiles):
            for x in range(n):
                a, b = (
                    p_ref[k, pl.ds(j * n + x, 8, stride=0), :] for j in (2 * g, 2 * g + 1)
                )
                p8[g, x, :, at(k)] = jnp.where(upper, a, b)
    for g in range(pairs):
        for x in range(0, n, 2):
            both = []
            for y in (x, x + 1):
                both.append(butterfly([t8[y, :, cls(s)] * p8[g, y, :, cls(s)] for s in range(4)]))
            q = slice((g * n + x) * 8, (g * n + x + 2) * 8)
            for s in range(4):
                gh[s, q, :], gl[s, q, :] = split(jnp.concatenate([both[0][s], both[1][s]], axis=0))

    def forward(s):
        ps[s] = dot(gh[s], w_ref[s]) + dot(gl[s], w_ref[s]) + dot(gh[s], w_ref[4 + s])

    def middle(s):
        for g in range(pairs):
            for h in range(quarter // LANES):
                v = [ps[s, (g * n + x) * 8 : (g * n + x + 1) * 8, at(h)] for x in range(n)]
                k = s * (quarter // LANES) + h
                v = along_x(v, lambda r, k=k: k_ref[k, pl.ds(r, 8, stride=0), :])
                for x in range(0, n, 2):
                    q = slice((g * n + x) * 8, (g * n + x + 2) * 8)
                    gh[s, q, at(h)], gl[s, q, at(h)] = split(jnp.concatenate(v[x : x + 2], axis=0))

    def back(s):
        ps[s] = dot_t(gh[s], w_ref[s]) + dot_t(gl[s], w_ref[s]) + dot_t(gh[s], w_ref[4 + s])

    steps = "ffffmmmmbbbb" if last else "ffmfmbfmbmbb"
    seen = dict.fromkeys("fmb", 0)
    for step in steps:
        {"f": forward, "m": middle, "b": back}[step](seen[step])
        seen[step] += 1
    done = []
    for x in range(n):
        acc = [prior[x, :, cls(s)] if last else None for s in range(4)]
        for g in range(pairs):
            q = slice((g * n + x) * 8, (g * n + x + 1) * 8)
            for s, v in enumerate(butterfly([ps[s, q, :] for s in range(4)])):
                v = v * p8[g, x, :, cls(s)]
                acc[s] = v if acc[s] is None else acc[s] + v
        if not last:
            for s in range(4):
                o_ref[x, :, cls(s)] = acc[s]
            continue
        done.append(acc)
        if len(done) == 2:
            folded = {}
            for s in range(4):
                for h in range(quarter // LANES):
                    a, b = (v[s][:, at(h)] for v in done)
                    folded[s, h] = jnp.where(upper, a, pltpu.roll(b, tb, 0)) + jnp.where(upper, pltpu.roll(a, tb, 0), b)
            for (c, h), v in folded.items():
                o_ref[x // 2, :, slice(quarter * c + LANES * h, quarter * c + LANES * (h + 1))] = v
            done = []


def solve(targets, partners, consts, prior=None):
    last = prior is not None
    tiles, rows, _ = partners.shape
    n, tb = 32, 4
    pairs = rows // n // 2
    vmem = pl.BlockSpec(memory_space=pltpu.VMEM)
    part = jax.ShapeDtypeStruct((n, 2 * tb, n * n), jnp.float32)
    if last:
        operands = (targets, prior, partners, *consts)
        out_shape = jax.ShapeDtypeStruct((n // 2, 2 * tb, n * n), jnp.float32)
    else:
        operands = (targets, partners, *consts)
        out_shape = (part, part)
    long = pairs * n * 2 * tb
    scratch = [
        pltpu.VMEM((pairs, n, 2 * tb, n * n), jnp.float32),
        pltpu.VMEM((4, long, n * n // 4), jnp.bfloat16),
        pltpu.VMEM((4, long, n * n // 4), jnp.bfloat16),
        pltpu.VMEM((4, long, n * n // 4), jnp.float32),
    ]
    if not last:
        scratch.append(pltpu.VMEM((tiles, tb * n, LANES), jnp.float32))
    return pl.pallas_call(
        functools.partial(solve_body, last, tb, n),
        out_shape=out_shape,
        in_specs=[vmem] * len(operands),
        out_specs=vmem if last else (vmem, vmem),
        scratch_shapes=scratch,
        compiler_params=SOLVE_PARAMS,
        cost_estimate=pl.CostEstimate(
            flops=2 * 6 * long * (n * n // 2) ** 2, bytes_accessed=8 << 20, transcendentals=0
        ),
    )(*operands)


def spread_body(in_ref, o_ref):
    peers, rows, _ = in_ref.shape
    halves = []
    for core in (0, 1):
        total = in_ref[core]
        for k in range(core + 2, peers, 2):
            total = total + in_ref[k]
        halves.append(total)
    order = [v[q * rows // 2 : (q + 1) * rows // 2] for q in (0, 1) for v in halves]
    slab = jnp.concatenate(order, axis=0)
    folded = {(k // 2, k % 2): slab[:, LANES * k : LANES * (k + 1)] for k in range(8)}
    slab = jnp.concatenate(unfold(folded, slab.shape[0]), axis=1)
    for k in range(o_ref.shape[0]):
        o_ref[k] = slab


def spread(received, copies):
    _, rows, plane = received.shape
    return pl.pallas_call(
        spread_body,
        out_shape=jax.ShapeDtypeStruct((copies, 2 * rows, plane), jnp.float32),
        compiler_params=SMALL_PARAMS,
    )(received)


def plane_of(ref, q):
    half = ref.shape[1] // 2
    return ref[:, q * half : (q + 1) * half, :].reshape(ref.shape[0] * half, ref.shape[2])


def overlap_body(scale, t_ref, a_ref, o_ref):
    owned = t_ref.shape[0]
    first = 2 * lax.axis_index(PTR)
    t = [
        jnp.concatenate([t_ref[i, pl.ds(first + q, 1), :] for i in range(owned)], axis=0) for q in (0, 1)
    ]
    total = scale * lax.dot_general(
        jnp.concatenate(t, axis=1),
        jnp.concatenate([plane_of(a_ref, q) for q in (0, 1)], axis=1),
        (((1,), (1,)), ((), ())),
        precision=lax.Precision.HIGHEST,
        preferred_element_type=jnp.float32,
    )
    packed = jnp.concatenate([total[: owned // 2], total[owned // 2 :]], axis=1)
    for k in range(o_ref.shape[0]):
        o_ref[k] = packed


def overlap(targets, slab, copies, scale):
    owned = targets.shape[0]
    count = slab.shape[0] * owned
    return pl.pallas_call(
        functools.partial(overlap_body, scale),
        out_shape=jax.ShapeDtypeStruct((copies, owned // 2, 2 * count), jnp.float32),
        compiler_params=SMALL_PARAMS,
    )(targets, slab)


def compress_body(owned, s_ref, a_ref, keep_ref, o_ref, inv_ref):
    groups = lax.axis_size(TGT)
    slabs = s_ref.shape[0] // groups
    count = groups * owned
    rows = []
    for t in range(groups):
        terms = [s_ref[t * slabs + k] for k in range(slabs)]
        while len(terms) > 1:
            terms = [a + b for a, b in zip(terms[0::2], terms[1::2])]
        total = terms[0]
        rows += [total[:, :count], total[:, count:]]
    square = jnp.concatenate(rows, axis=0)
    square = 0.5 * (square + square.T)
    row = lax.broadcasted_iota(jnp.int32, (count, count), 0)
    col = lax.broadcasted_iota(jnp.int32, (count, count), 1)
    wide = jnp.concatenate([square, jnp.where(row == col, 1.0, 0.0)], axis=1)
    tiles = [wide[8 * t : 8 * t + 8] for t in range(count // 8)]
    sub = lax.broadcasted_iota(jnp.int32, (8, LANES), 0)
    down = lambda v, k: jnp.broadcast_to(v[k : k + 1], (8, LANES))
    wide_panel = 16
    tops = count // 8
    roots = [jnp.ones((8, LANES), jnp.float32)] * tops
    for p in range(0, count, wide_panel):
        cols = {
            (t, k): jnp.broadcast_to(tiles[t][:, k : k + 1], (8, LANES))
            for t in range(p // 8, tops)
            for k in range(p, p + wide_panel)
        }
        for k in range(p, p + wide_panel, 2):
            top, r = k // 8, k % 8
            one, two = cols[top, k], cols[top, k + 1]
            a, b, d = down(one, r), down(two, r), down(two, r + 1)
            over = 1.0 / a
            under = a * (1.0 / (a * d - b * b))
            ratio = b * over
            pivot = d - b * ratio
            roots[top] = jnp.where(sub == r, lax.rsqrt(a), jnp.where(sub == r + 1, lax.rsqrt(pivot), roots[top]))
            line = down(tiles[top], r)
            next_line = down(tiles[top], r + 1) - ratio * line
            rest = range(k + 2, p + wide_panel)
            cross = {m: (down(cols[top, m], r), down(cols[top, m], r + 1)) for m in rest}
            cross = {m: (u, v - ratio * u) for m, (u, v) in cross.items()}
            for t in range(top, tops):
                f = cols[t, k] * over
                g = (cols[t, k + 1] - cols[t, k] * ratio) * under
                if t == top:
                    f = jnp.where(sub > r, f, 0.0)
                    g = jnp.where(sub > r + 1, g, 0.0)
                tiles[t] = tiles[t] - f * line - g * next_line
                for m in rest:
                    u, v = cross[m]
                    cols[t, m] = cols[t, m] - f * u - g * v
    for t in range(tops):
        inv_ref[8 * t : 8 * t + 8, :] = tiles[t] * roots[t]
    first = lax.axis_index(TGT) * owned
    mine = inv_ref[pl.ds(pl.multiple_of(first, 8), owned), :][:, count:]
    kept = first + lax.broadcasted_iota(jnp.int32, (owned, count), 0) < keep_ref[:owned, :count]
    mine = jnp.where(kept, mine, 0.0)
    both = jnp.dot(
        mine,
        jnp.concatenate([plane_of(a_ref, q) for q in (0, 1)], axis=1),
        precision=lax.Precision.HIGHEST,
        preferred_element_type=jnp.float32,
    )
    for q in (0, 1):
        o_ref[:, q, :] = both[:, q * a_ref.shape[2] : (q + 1) * a_ref.shape[2]]


def compress(summands, slab, keep, owned):
    count = slab.shape[0] * owned
    vmem = pl.BlockSpec(memory_space=pltpu.VMEM)
    return pl.pallas_call(
        functools.partial(compress_body, owned),
        out_shape=jax.ShapeDtypeStruct((owned, 2, slab.shape[2]), jnp.float32),
        in_specs=[vmem] * 3,
        out_specs=vmem,
        scratch_shapes=[pltpu.VMEM((count, LANES), jnp.float32)],
        compiler_params=SMALL_PARAMS,
    )(summands, slab, keep)


def shards(targets, partners, occupied, retained):
    owned, n, plane = targets.shape
    consts = [jnp.asarray(c) for c in tables(n)]
    groups = lax.axis_size(TGT)
    swap = [(0, 1), (1, 0)]
    own_partners, keep = folded_partners(partners, occupied, retained)
    other_partners = lax.ppermute(own_partners, "core", swap)
    partial_actions, folded = solve(targets, own_partners, consts)
    cut = solve(folded, other_partners, consts, partial_actions)
    copies = spread(lax.all_to_all(cut, PTR, 0, 0, tiled=True), groups)
    slab = lax.all_to_all(copies, TGT, 0, 0, tiled=True)
    summands = overlap(targets, slab, lax.axis_size(TGT + PTR), 1.0 / n**3)
    summands = lax.all_to_all(summands, TGT + PTR, 0, 0, tiled=True)
    return compress(summands, slab, keep, owned)


def solution(mesh):
    names = TGT + PTR
    finer = Mesh(mesh.devices.reshape(2, 4, 4, 2, 2), names)
    in_specs = (P(TGT, None, None), P(None, None, PTR), P(PTR), P())
    out_specs = P(TGT, PTR, None)
    return jax.shard_map(
        shards, mesh=finer, in_specs=in_specs, out_specs=out_specs, check_vma=False
    )
```
